32 devices in a mesh: dp: 16 (over z, y, x), tile: 2 (over core).
Axes of the slice: x: 2, y: 2, z: 4, core: 2. Of those that a mesh axis runs over, the one named last changes fastest.
Arguments:
- snapshots: bfloat16 [8208, 3, 32, 128], P('dp', None, 'tile'), may hold values from -16 to 16, as said below
- pair_start: int32 [8192], P('dp'), may hold values from 0 to 511
- bath_class: int32 [32, 128], P('tile'), may hold values from 0 to 3
- stencil_w: float32 [3, 3, 3, 9], replicated, may hold values from -1.25 to 1.25
- depth_gain: float32 [3, 4], replicated, may hold values from 0.5 to 2
- stencil_bias: float32 [3, 3], replicated, may hold values from -2 to 2
- readout: float32 [3], replicated, may hold values from -3.5 to 3.5
- panel_order: int32 [8], replicated, may hold values from 0 to 7, each once
Outputs:
- chol_panels: float32 [2, 2048, 1024], P('tile', 'dp')
- cross_whitened: float32 [2, 2048, 1024], P('tile', 'dp')
- ridge_shift: float32 [], replicated
The draws below stay inside these ranges and needn't reach their ends.
Inputs may be any that keep to these rules, and one draw needn't show every extreme that they name: snapshots stay within the range. The pair's second snapshot is the next one, pair_start + 1, of the same index of dp. `panel_order`: each block number appears once.
All inputs are finite; a program needn't handle non-finite values.
Results may differ from the reference program's by a relative error of at most 0.0032.
Values may be sent and summed in bfloat16 or wider, within the bound.
No kernel may reach another device: no remote copies, remote signals or barrier semaphores. Data moves between devices by JAX's collectives and lax.ppermute only.
A program may use at most 192 MiB of HBM per device.

```python
import math
import jax
import jax.numpy as jnp
from jax import lax

GRID_ROWS = 32
GRID_COLS = 128
NFIELD = 3
LAYERS = 3
NCLASS = 4
NBLK = 8
PAIRS_DEV = 512
SNAP_DEV = 513
SNAPS = 8208
PAIRS = 8192
OBS = 4096
PANEL = 512
N_DP = 16
N_TILE = 2


def draw_snapshots(key, part):
    key_base, key_snap, key_cell = jax.random.split(key, 3)
    shape = (SNAPS, NFIELD, GRID_ROWS, GRID_COLS)
    position = jnp.arange(SNAPS, dtype=jnp.float32) / float(max(SNAPS - 1, 1))
    base = jnp.clip(jax.random.normal(key_base, shape, jnp.float32), -4.0, 4.0)
    rising = 1.0 + 2.0 * position
    snap_scale = rising * jnp.exp(jax.random.uniform(key_snap, (SNAPS,), jnp.float32, math.log(0.3), 0.0))
    cell_scale = jnp.exp(jax.random.uniform(key_cell, (GRID_ROWS, GRID_COLS), jnp.float32, math.log(0.4), math.log(1.25)))
    values = base * snap_scale[:, None, None, None] * cell_scale[None, None]
    return values.astype(jnp.bfloat16)


def with_ends(entries, stream_key, least, largest):
    shape = entries.shape
    index_at = [jax.random.randint(jax.random.fold_in(stream_key, axis), (), 0, shape[axis]) for axis in range(len(shape))]
    entries = entries.at[tuple(index_at)].set(least)
    longest = shape.index(max(shape))
    index_at[longest] = (index_at[longest] + 1) % shape[longest]
    return entries.at[tuple(index_at)].set(largest)


def bell_draw(own_key, extent, scale, limit, kind=jnp.bfloat16):
    values = jax.random.normal(own_key, extent, jnp.float32) * scale
    return jnp.minimum(jnp.maximum(values, -limit), limit).astype(kind)


def setup_inputs(seed: int = 0) -> dict:
    streams_of = jax.random.split(jax.random.key(seed), 9)
    return {
        "snapshots": draw_snapshots(jax.random.fold_in(streams_of[8], 71), 0),
        "pair_start": with_ends(jax.random.randint(streams_of[1], (PAIRS,), 0, SNAP_DEV - 1), jax.random.fold_in(streams_of[1], 1), 0, (SNAP_DEV - 1) - 1).astype(jnp.int32),
        "bath_class": with_ends(jax.random.randint(streams_of[2], (GRID_ROWS, GRID_COLS), 0, NCLASS), jax.random.fold_in(streams_of[2], 1), 0, NCLASS - 1).astype(jnp.int32),
        "stencil_w": bell_draw(streams_of[3], (LAYERS, NFIELD, NFIELD, 9), (NFIELD * 9) ** -0.5, 1.25, jnp.float32),
        "depth_gain": jnp.clip(jnp.exp(jax.random.uniform(streams_of[4], (LAYERS, NCLASS), jnp.float32, math.log(0.5), math.log(2.0))), 0.5, 2.0),
        "stencil_bias": bell_draw(streams_of[5], (LAYERS, NFIELD), 0.5, 2.0, jnp.float32),
        "readout": bell_draw(streams_of[6], (NFIELD,), NFIELD ** -0.5, 3.5, jnp.float32),
        "panel_order": jax.random.permutation(streams_of[7], NBLK).astype(jnp.int32),
    }


ridge_factor = 0.5

def gain_field(classes, gains):
    field = jnp.zeros(classes.shape, jnp.float32)
    for class_idx in range(gains.shape[0]):
        field = field + jnp.where(classes == class_idx, gains[class_idx], jnp.zeros((), jnp.float32))
    return field

def layer_step(padded_rows, gains_map, weights, bias):
    wide = jnp.pad(padded_rows, ((0, 0), (0, 0), (0, 0), (1, 1)))
    out_rows = padded_rows.shape[2] - 2
    width_cols = padded_rows.shape[3]
    fields_count = padded_rows.shape[1]
    stencil_sum = jnp.zeros((padded_rows.shape[0], fields_count, out_rows, width_cols), jnp.float32)
    for row_off in range(3):
        for col_off in range(3):
            offset = row_off * 3 + col_off
            moved = wide[:, :, row_off:row_off + out_rows, col_off:col_off + width_cols]
            for source in range(fields_count):
                stencil_sum = stencil_sum + weights[:, source, offset][None, :, None, None] * moved[:, source:source + 1]
    centre = padded_rows[:, :, 1:-1, :]
    return centre + jnp.tanh(gains_map[None, None] * stencil_sum + bias[None, :, None, None])

def readout_sum(fields, readout):
    result = jnp.zeros((fields.shape[0], fields.shape[2], fields.shape[3]), jnp.float32)
    for field_idx in range(fields.shape[1]):
        result = result + readout[field_idx] * fields[:, field_idx]
    return result

def encode(snap_block, bath_class, stencil_w, depth_gain, stencil_bias, readout):
    fields = snap_block.astype(jnp.float32)
    for layer_idx in range(LAYERS):
        padded = jnp.pad(fields, ((0, 0), (0, 0), (1, 1), (0, 0)))
        fields = layer_step(padded, gain_field(bath_class, depth_gain[layer_idx]), stencil_w[layer_idx], stencil_bias[layer_idx])
    mixed = readout_sum(fields, readout)
    return mixed.reshape(mixed.shape[0], GRID_ROWS * GRID_COLS).astype(jnp.bfloat16)

def right_solve(lower_factor, rows_in):
    return lax.linalg.triangular_solve(lower_factor, rows_in, left_side=False, lower=True, transpose_a=True)

def panel_factor(diag_rows):
    lead = jnp.linalg.cholesky(diag_rows[:PANEL, :PANEL])
    below = right_solve(lead, diag_rows[PANEL:, :PANEL])
    rest = diag_rows[PANEL:, PANEL:] - jnp.dot(below, below.T, precision=lax.Precision.HIGHEST)
    tail = jnp.linalg.cholesky(rest)
    return (lead, below, tail)

def apply_factor(rows_in, lead, below, tail):
    left = right_solve(lead, rows_in[:, :PANEL])
    inner = rows_in[:, PANEL:] - jnp.dot(left, below.T, precision=lax.Precision.HIGHEST)
    right = right_solve(tail, inner)
    return jnp.concatenate([left, right], axis=1)

def reference(snapshots, pair_start, bath_class, stencil_w, depth_gain, stencil_bias, readout, panel_order):
    width = 2 * PANEL
    first_block = panel_order[0].astype(jnp.int32)
    second_block = panel_order[1].astype(jnp.int32)
    snap_blocks = snapshots.reshape(N_DP, SNAP_DEV, NFIELD, GRID_ROWS, GRID_COLS)
    start_blocks = pair_start.reshape(N_DP, PAIRS_DEV)

    def accumulate(carry, inputs):
        gram, cross, energy = carry
        snap_block, start_block = inputs
        encoded = encode(snap_block, bath_class, stencil_w, depth_gain, stencil_bias, readout)
        earlier = jnp.take(encoded, start_block, axis=0)
        later = jnp.take(encoded, start_block + 1, axis=0)
        panel = jnp.concatenate([lax.dynamic_slice_in_dim(earlier, first_block * PANEL, PANEL, 1), lax.dynamic_slice_in_dim(earlier, second_block * PANEL, PANEL, 1)], axis=1)
        dims = (((0,), (0,)), ((), ()))
        gram = gram + lax.dot_general(earlier.astype(jnp.float32), panel.astype(jnp.float32), dims, preferred_element_type=jnp.float32)
        cross = cross + lax.dot_general(later.astype(jnp.float32), panel.astype(jnp.float32), dims, preferred_element_type=jnp.float32)
        energy = energy + jnp.sum(jnp.square(earlier.astype(jnp.float32)))
        return ((gram, cross, energy), None)
    start_carry = (jnp.zeros((OBS, width), jnp.float32), jnp.zeros((OBS, width), jnp.float32), jnp.zeros((), jnp.float32))
    (gram, cross, energy), unused = lax.scan(accumulate, start_carry, (snap_blocks, start_blocks))
    pairs_total = float(PAIRS_DEV * N_DP)
    gram = gram / pairs_total
    cross = cross / pairs_total
    shift_value = ridge_factor * (energy / pairs_total) / float(OBS)
    row_obs = jnp.arange(OBS, dtype=jnp.int32)[:, None]
    col_obs = jnp.concatenate([first_block * PANEL + jnp.arange(PANEL, dtype=jnp.int32), second_block * PANEL + jnp.arange(PANEL, dtype=jnp.int32)])[None, :]
    shifted = gram + shift_value * (row_obs == col_obs).astype(jnp.float32)
    diag_rows = jnp.concatenate([lax.dynamic_slice_in_dim(shifted, first_block * PANEL, PANEL, 0), lax.dynamic_slice_in_dim(shifted, second_block * PANEL, PANEL, 0)], axis=0)
    lead, below, tail = panel_factor(diag_rows)
    factor = apply_factor(shifted, lead, below, tail)
    panel_full = jnp.concatenate([jnp.concatenate([lead, jnp.zeros_like(lead)], axis=1), jnp.concatenate([below, tail], axis=1)], axis=0)
    zero_index = jnp.zeros((), jnp.int32)
    factor = lax.dynamic_update_slice(factor, panel_full[:PANEL], (first_block * PANEL, zero_index))
    factor = lax.dynamic_update_slice(factor, panel_full[PANEL:], (second_block * PANEL, zero_index))
    whitened = apply_factor(cross, lead, below, tail)
    return (factor.reshape(N_TILE, OBS // N_TILE, width), whitened.reshape(N_TILE, OBS // N_TILE, width), shift_value)
```

```python
import jax
import jax.numpy as jnp
from jax import lax
from jax.experimental import pallas as pl
from jax.experimental.pallas import tpu as pltpu
from jax.sharding import PartitionSpec as P

F32 = jnp.float32
BF16 = jnp.bfloat16


EDGE = 128
PANEL = 512


def halo_kernel(tile_ref, own_ref, out_ref):
    block = own_ref.shape[0]
    row = lax.broadcasted_iota(jnp.int32, (16, 48), 0)
    col = lax.broadcasted_iota(jnp.int32, (16, 48), 1)
    dist = lax.div(row, 3)
    source = jnp.where(tile_ref[0] == 0, 15 - dist, dist)
    pick = jnp.where((row < 9) & (col == lax.rem(row, 3) * 16 + source), 1.0, 0.0).astype(BF16)
    for base in range(0, block, 3):
        cells = jnp.concatenate(
            [own_ref[base + k].reshape(48, 128) for k in range(3)], axis=1
        )
        rows = jnp.dot(pick, cells, preferred_element_type=F32).astype(BF16)
        for k in range(3):
            out_ref[base + k] = rows[:, 128 * k : 128 * (k + 1)]


def halo_rows(tile_idx, snapshots):
    count = snapshots.shape[0]
    block = next(b for b in (57, 27, 9, 3) if count % b == 0)
    return pl.pallas_call(
        halo_kernel,
        grid=(count // block,),
        in_specs=[
            pl.BlockSpec(memory_space=pltpu.SMEM),
            pl.BlockSpec((block, 3, 16, 128), lambda i: (i, 0, 0, 0)),
        ],
        out_specs=pl.BlockSpec((block, 16, 128), lambda i: (i, 0, 0)),
        out_shape=jax.ShapeDtypeStruct((count, 16, 128), BF16),
        name="halo_rows",
    )(tile_idx, snapshots)


GROUP = 32
BLOCK = 32


def encode_kernel(
    tile_ref, w_ref, gain_ref, bias_ref, readout_ref,
    own_ref, halo_ref, cls_ref, ncls_ref, out_ref,
    mat_ref, gmap_ref, bmap_ref, enc_ref, *, count,
):
    @pl.when(pl.program_id(0) == 0)
    def _():
        tile = tile_ref[0]
        r_out = lax.broadcasted_iota(jnp.int32, (56, 64), 0)
        r_in = lax.broadcasted_iota(jnp.int32, (56, 64), 1)

        def place(r):
            h = r - 48
            outside = jnp.where(tile == 0, 16 + lax.div(h, 3), -1 - lax.div(h, 3))
            return jnp.where(r < 48, lax.div(r, 16), lax.rem(h, 3)), jnp.where(r < 48, lax.rem(r, 16), outside)

        o_idx, o_pos = place(r_out)
        i_idx, i_pos = place(r_in)
        tap = i_pos - o_pos + 1
        good = (tap >= 0) & (tap <= 2) & (r_in < 57) & (r_out < 54)
        code = jnp.where(good, (o_idx * 3 + i_idx) * 3 + tap, -1)
        hits = [code == k for k in range(27)]
        for layer in range(3):
            for b in range(3):
                acc = jnp.zeros((56, 64), F32)
                for k in range(27):
                    weight = w_ref[((layer * 9 + k // 3) * 3 + k % 3) * 3 + b]
                    acc = jnp.where(hits[k], weight, acc)
                high = acc.astype(BF16).astype(F32)
                low = acc - high
                full = jnp.concatenate([high, low, high], axis=1).astype(BF16)
                mat_ref[layer, 56 * b : 56 * (b + 1), :] = full
        own_cls = cls_ref[...]
        near = ncls_ref[...]
        h0 = jnp.where(tile == 0, near[0:1], near[15:16])
        h1 = jnp.where(tile == 0, near[1:2], near[14:15])
        cls = jnp.concatenate([own_cls] * 3 + [h0, h0, h0, h1, h1, h1, h1, h1], axis=0)
        row = lax.broadcasted_iota(jnp.int32, (56, 128), 0)
        field = jnp.where(row < 48, lax.div(row, 16), lax.rem(row - 48, 3))
        for layer in range(3):
            gmap = jnp.zeros((56, 128), F32)
            for c in range(4):
                gmap = jnp.where(cls == c, gain_ref[layer * 4 + c], gmap)
            gmap_ref[layer] = gmap
            bmap = jnp.zeros((56, 128), F32)
            for f in range(3):
                bmap = jnp.where(field == f, bias_ref[layer * 3 + f], bmap)
            bmap_ref[layer] = bmap

    lane = lax.broadcasted_iota(jnp.int32, (56, 128), 1)
    first_lane = lane == 0
    last_lane = lane == 127
    blank = jnp.zeros((8, 128), F32)
    ro = [readout_ref[f] for f in range(3)]

    def group(g, carry):
        base = g * GROUP
        high = []
        low = []
        fields = []
        for k in range(GROUP):
            own = own_ref[base + k].reshape(48, 128)
            halo = halo_ref[base + k]
            high.append(jnp.concatenate([own, halo], axis=0))
            fields.append(
                jnp.concatenate([own.astype(F32), halo.astype(F32)[:8]], axis=0)
            )
        for layer in range(3):
            top = jnp.concatenate(high, axis=1)
            if layer == 0:
                stacked = jnp.concatenate([top, top], axis=0)
                mat = mat_ref[layer, :, 0:128]
            else:
                stacked = jnp.concatenate([top, top, jnp.concatenate(low, axis=1)], axis=0)
                mat = mat_ref[layer]
            sums = jnp.dot(mat, stacked, preferred_element_type=F32)
            high = []
            low = []
            for k in range(GROUP):
                part = sums[:, 128 * k : 128 * (k + 1)]
                left = jnp.where(first_lane, 0.0, pltpu.roll(part[0:56], 1, 1))
                right = jnp.where(last_lane, 0.0, pltpu.roll(part[112:168], 127, 1))
                total = left + part[56:112] + right
                fields[k] = fields[k] + jnp.tanh(gmap_ref[layer] * total + bmap_ref[layer])
                if layer < 2:
                    wide = jnp.concatenate([fields[k], blank], axis=0)
                    upper = wide.astype(BF16)
                    high.append(upper)
                    low.append((wide - upper.astype(F32)).astype(BF16))
        for k in range(GROUP):
            f = fields[k]
            value = ro[0] * f[0:16] + ro[1] * f[16:32] + ro[2] * f[32:48]
            enc_ref[pl.ds((base + k) * 16, 16), :] = value
        return carry

    lax.fori_loop(0, BLOCK // GROUP, group, 0, unroll=True)
    snap = lax.broadcasted_iota(jnp.int32, (BLOCK, 128), 0) + pl.program_id(0) * BLOCK
    for r in range(16):
        rows = enc_ref[pl.ds(r, BLOCK, stride=16), :]
        out_ref[r] = jnp.where(snap < count, rows, 0.0).astype(BF16)


def encode(tile_idx, snapshots, halo, classes, near_classes, stencil_w, depth_gain, bias, readout):
    count = snapshots.shape[0]
    smem = pl.BlockSpec(memory_space=pltpu.SMEM)
    whole = pl.BlockSpec((16, 128), lambda i: (0, 0))

    def body(*refs):
        encode_kernel(*refs, count=count)

    return pl.pallas_call(
        body,
        grid=(pl.cdiv(count, BLOCK),),
        in_specs=[
            smem, smem, smem, smem, smem,
            pl.BlockSpec((BLOCK, 3, 16, 128), lambda i: (i, 0, 0, 0)),
            pl.BlockSpec((BLOCK, 16, 128), lambda i: (i, 0, 0)),
            whole, whole,
        ],
        out_specs=pl.BlockSpec((16, BLOCK, 128), lambda i: (0, i, 0)),
        out_shape=jax.ShapeDtypeStruct((16, pl.cdiv(count, BLOCK) * BLOCK, 128), BF16),
        scratch_shapes=[
            pltpu.VMEM((3, 168, 192), BF16),
            pltpu.VMEM((3, 56, 128), F32),
            pltpu.VMEM((3, 56, 128), F32),
            pltpu.VMEM((BLOCK * 16, 128), F32),
        ],
        name="encode",
    )(
        tile_idx, stencil_w.reshape(-1), depth_gain.reshape(-1), bias.reshape(-1), readout,
        snapshots, halo, classes, near_classes,
    )


def split(x):
    high = x.astype(BF16)
    return high, (x - high.astype(F32)).astype(BF16)


def lhs3(x):
    high, low = split(x)
    return jnp.concatenate([high, high, low], axis=1)


def rhs3(x):
    high, low = split(x)
    return jnp.concatenate([high, low, high], axis=1)


def dot_nt(a, b):
    return lax.dot_general(a, b, (((1,), (1,)), ((), ())), preferred_element_type=F32)


def factor_diag(block, eye):
    row8 = lax.broadcasted_iota(jnp.int32, (8, EDGE), 0)
    groups = EDGE // 8
    a = [block[8 * g : 8 * (g + 1)] for g in range(groups)]
    b = [eye[8 * g : 8 * (g + 1)] for g in range(groups)]
    for j in range(EDGE):
        home, inner = divmod(j, 8)
        row = jnp.broadcast_to(a[home][inner : inner + 1, :], (8, EDGE))
        pivot = jnp.broadcast_to(row[:, j : j + 1], (8, EDGE))
        invert = 1.0 / pivot
        scaled = row * invert
        brow = jnp.broadcast_to(b[home][inner : inner + 1, :], (8, EDGE)) * invert
        for g in range(home, groups):
            if g == home and inner == 7:
                continue
            col = jnp.broadcast_to(a[g][:, j : j + 1], (8, EDGE))
            if g == home:
                col = jnp.where(row8 > inner, col, 0.0)
            a[g] = a[g] - col * scaled
            b[g] = b[g] - col * brow
    return jnp.concatenate(a, axis=0), jnp.concatenate(b, axis=0)


def pick_kernel(start_ref, enc_ref, keep_ref, near_ref, out_ref):
    snaps = enc_ref.shape[1]
    pairs = start_ref.shape[1]
    snap_idx = lax.broadcasted_iota(jnp.int32, (snaps, pairs), 0)
    hit = jnp.where(snap_idx == start_ref[...], 1.0, 0.0).astype(BF16)
    panel = jnp.concatenate(
        [keep_ref[r] + near_ref[r] for r in range(keep_ref.shape[0])], axis=1
    )
    tn = (((0,), (0,)), ((), ()))
    out_ref[0:PANEL, :] = lax.dot_general(
        panel, hit, tn, preferred_element_type=F32
    ).astype(BF16)
    norms = jnp.zeros(enc_ref.shape[1:], F32)
    for r in range(enc_ref.shape[0]):
        value = enc_ref[r].astype(F32)
        norms = norms + value * value
    total = jnp.zeros((enc_ref.shape[2], pairs), F32)
    for _ in range(3):
        high = norms.astype(BF16)
        total = total + lax.dot_general(high, hit, tn, preferred_element_type=F32)
        norms = norms - high.astype(F32)
    total = jnp.sum(jnp.sum(total, axis=0, keepdims=True), axis=1, keepdims=True)
    rest = jnp.broadcast_to(total, (16, pairs))
    row = lax.broadcasted_iota(jnp.int32, (16, pairs), 0)
    packed = jnp.zeros((16, pairs), BF16)
    for k in range(3):
        high = rest.astype(BF16)
        packed = jnp.where(row == k, high.astype(F32), packed.astype(F32)).astype(BF16)
        rest = rest - high.astype(F32)
    out_ref[PANEL:, :] = packed


def pick(starts, enc, keep, near):
    pairs = starts.shape[1]
    return pl.pallas_call(
        pick_kernel,
        out_shape=jax.ShapeDtypeStruct((PANEL + 16, pairs), BF16),
        compiler_params=pltpu.CompilerParams(vmem_limit_bytes=40 * 2**20),
        name="pick_pairs",
    )(starts, enc, keep, near)


def factor_kernel(tile_ref, mine_ref, near_ref, low_ref, inv_ref, shift_ref, *, pairs_total, obs):
    step = pl.program_id(0)
    width = 2 * PANEL

    @pl.when(step == 0)
    def _():
        low_ref[...] = jnp.zeros((width, width), F32)
        shift_ref[...] = jnp.zeros(shift_ref.shape, F32)

    flip = tile_ref[0] == 1
    mine = mine_ref[0, 0:PANEL, :]
    near = near_ref[0, 0:PANEL, :]
    lead = jnp.where(flip, near, mine)
    tail = jnp.where(flip, mine, near)
    low_ref[0:PANEL, 0:PANEL] += dot_nt(lead, lead)
    low_ref[PANEL:, 0:PANEL] += dot_nt(tail, lead)
    low_ref[PANEL:, PANEL:] += dot_nt(tail, tail)
    parts = mine_ref[0, PANEL:, 0:128].astype(F32) + 0.0
    parts_near = near_ref[0, PANEL:, 0:128].astype(F32) + 0.0
    both = jnp.sum(parts, axis=0, keepdims=True) + jnp.sum(parts_near, axis=0, keepdims=True)
    shift_ref[...] += jnp.broadcast_to(both, shift_ref.shape)

    @pl.when(step == pl.num_programs(0) - 1)
    def _():
        shift = 0.5 * (shift_ref[...] / pairs_total) / float(obs)
        shift_ref[...] = shift
        factor(low_ref, inv_ref, shift, 1.0 / pairs_total)


def factor(low_ref, inv_ref, shift, scale):
    width = low_ref.shape[0]
    row = lax.broadcasted_iota(jnp.int32, (EDGE, EDGE), 0)
    col = lax.broadcasted_iota(jnp.int32, (EDGE, EDGE), 1)
    eye = jnp.where(row == col, 1.0, 0.0)
    blocks = width // EDGE
    shift_wide = jnp.concatenate([shift] * (EDGE // 8), axis=0)

    for i in range(blocks):
        rows = pl.ds(EDGE * i, EDGE)
        low_ref[rows, :] = low_ref[rows, :] * scale
        low_ref[rows, EDGE * i : EDGE * (i + 1)] += jnp.where(row == col, shift_wide, 0.0)
        if EDGE * (i + 1) < width:
            low_ref[rows, EDGE * (i + 1) :] = jnp.zeros((EDGE, width - EDGE * (i + 1)), F32)

    def update(k):
        here = EDGE * k
        rest = EDGE * (k + 1)
        below = dot_nt(lhs3(low_ref[rest:, here:rest]), rhs3(inv_ref[here:rest, :]))
        low_ref[rest:, here:rest] = below
        left = lhs3(below)
        right = rhs3(below)
        start = rest
        while start < width:
            stop = start + (2 * EDGE if (width - start) % (2 * EDGE) == 0 else EDGE)
            low_ref[start:, start:stop] -= dot_nt(
                left[start - rest :], right[start - rest : stop - rest]
            )
            start = stop

    def step(k, carry):
        at = pl.ds(pl.multiple_of(k * EDGE, EDGE), EDGE)
        upper, unit = factor_diag(low_ref[at, at], eye)
        pivots = jnp.sum(jnp.where(row == col, upper, 0.0), axis=1, keepdims=True)
        root = lax.rsqrt(pivots)
        low_ref[at, at] = (jnp.where(col >= row, upper, 0.0) * root).T
        inv_ref[at, :] = unit * root
        for static in range(blocks - 1):
            @pl.when(k == static)
            def _():
                update(static)
        return carry

    lax.fori_loop(0, blocks, step, 0)
    for i in range(blocks - 1):
        low_ref[EDGE * i : EDGE * (i + 1), EDGE * (i + 1) : EDGE * (i + 2)] = jnp.zeros((EDGE, EDGE), F32)


def gram_factor(tile_idx, mine, near, obs):
    steps, rows, pairs = mine.shape
    width = 2 * PANEL
    piece = pl.BlockSpec((1, rows, pairs), lambda i: (i, 0, 0))

    def body(*refs):
        factor_kernel(*refs, pairs_total=float(steps * pairs), obs=obs)

    return pl.pallas_call(
        body,
        grid=(steps,),
        in_specs=[pl.BlockSpec(memory_space=pltpu.SMEM), piece, piece],
        out_specs=[
            pl.BlockSpec((width, width), lambda i: (0, 0)),
            pl.BlockSpec((width, EDGE), lambda i: (0, 0)),
            pl.BlockSpec((8, EDGE), lambda i: (0, 0)),
        ],
        out_shape=[
            jax.ShapeDtypeStruct((width, width), F32),
            jax.ShapeDtypeStruct((width, EDGE), F32),
            jax.ShapeDtypeStruct((8, EDGE), F32),
        ],
        compiler_params=pltpu.CompilerParams(vmem_limit_bytes=48 * 2**20),
        name="gram_factor",
    )(tile_idx, mine, near)


def rows_kernel(
    info_ref, start_ref, enc_ref, mine_ref, near_ref, low_ref, inv_ref,
    chol_ref, white_ref, sums_ref, *, pairs_total,
):
    step = pl.program_id(0)
    own = chol_ref.shape[0]
    width = 2 * PANEL

    @pl.when(step == 0)
    def _():
        sums_ref[...] = jnp.zeros(sums_ref.shape, F32)

    snaps = enc_ref.shape[1]
    pairs = start_ref.shape[2]
    snap_idx = lax.broadcasted_iota(jnp.int32, (snaps, pairs), 0)
    starts = start_ref[0]
    first = jnp.where(snap_idx == starts, 1.0, 0.0).astype(BF16)
    second = jnp.where(snap_idx == starts + 1, 1.0, 0.0).astype(BF16)
    tn = (((0,), (0,)), ((), ()))
    picked = jnp.concatenate(
        [
            lax.dot_general(enc_ref[0], first, tn, preferred_element_type=F32),
            lax.dot_general(enc_ref[0], second, tn, preferred_element_type=F32),
        ],
        axis=0,
    ).astype(BF16)
    flip = info_ref[0] == 1
    mine = mine_ref[0, 0:PANEL, :]
    near = near_ref[0, 0:PANEL, :]
    sums_ref[:, 0:PANEL] += dot_nt(picked, jnp.where(flip, near, mine))
    sums_ref[:, PANEL:] += dot_nt(picked, jnp.where(flip, mine, near))

    @pl.when(step == pl.num_programs(0) - 1)
    def _():
        sums_ref[...] = sums_ref[...] * (1.0 / pairs_total)
        for k in range(width // EDGE):
            here = EDGE * k
            rest = EDGE * (k + 1)
            solved = dot_nt(lhs3(sums_ref[:, here:rest]), rhs3(inv_ref[here:rest, :]))
            sums_ref[:, here:rest] = solved
            if rest < width:
                sums_ref[:, rest:] -= dot_nt(lhs3(solved), rhs3(low_ref[rest:, here:rest]))
        offset = info_ref[3]
        first_rows = low_ref[pl.ds(pl.multiple_of(offset, 8), own), :]
        second_rows = low_ref[pl.ds(pl.multiple_of(PANEL + offset, 8), own), :]
        chol_ref[...] = jnp.where(
            info_ref[1] == 1,
            first_rows,
            jnp.where(info_ref[2] == 1, second_rows, sums_ref[0:own, :]),
        )
        white_ref[...] = sums_ref[own:, :]


def whiten_rows(info, starts, enc, mine, near, low, inv):
    steps, snaps, own = enc.shape
    pairs = mine.shape[2]
    width = 2 * PANEL
    piece = pl.BlockSpec((1, mine.shape[1], pairs), lambda i: (i, 0, 0))

    def body(*refs):
        rows_kernel(*refs, pairs_total=float(steps * pairs))

    return pl.pallas_call(
        body,
        grid=(steps,),
        in_specs=[
            pl.BlockSpec(memory_space=pltpu.SMEM),
            pl.BlockSpec((1, 1, pairs), lambda i: (i, 0, 0)),
            pl.BlockSpec((1, snaps, own), lambda i: (i, 0, 0)),
            piece,
            piece,
            pl.BlockSpec((width, width), lambda i: (0, 0)),
            pl.BlockSpec((width, EDGE), lambda i: (0, 0)),
        ],
        out_specs=[
            pl.BlockSpec((own, width), lambda i: (0, 0)),
            pl.BlockSpec((own, width), lambda i: (0, 0)),
        ],
        out_shape=[jax.ShapeDtypeStruct((own, width), F32)] * 2,
        scratch_shapes=[pltpu.VMEM((2 * own, width), F32)],
        compiler_params=pltpu.CompilerParams(vmem_limit_bytes=48 * 2**20),
        name="whiten_rows",
    )(info, starts, enc, mine, near, low, inv)


def on_device(
    snapshots, pair_start, bath_class, stencil_w, depth_gain, stencil_bias, readout, panel_order
):
    tile_pos = lax.axis_index("tile")
    dp_pos = lax.axis_index("dp")
    tile_count = lax.axis_size("tile")
    dp_count = lax.axis_size("dp")
    grid_rows, grid_cols = bath_class.shape
    tile_obs = grid_rows * grid_cols
    own_rows = tile_obs // dp_count
    swap = [(0, 1), (1, 0)]
    tile_idx = tile_pos[None].astype(jnp.int32)

    starts = lax.all_gather(pair_start, "dp", axis=0, tiled=False)[:, None, :]
    near_class = lax.ppermute(bath_class, "tile", swap)
    halo = lax.ppermute(halo_rows(tile_idx, snapshots), "tile", swap)
    encoded = encode(
        tile_idx, snapshots, halo, bath_class, near_class,
        stencil_w, depth_gain, stencil_bias, readout,
    )
    snaps = encoded.shape[1]

    block_rows = PANEL // grid_cols
    tile_blocks = tile_obs // PANEL

    def block_part(block):
        at = (block % tile_blocks) * block_rows
        part = lax.dynamic_slice_in_dim(encoded, at, block_rows, 0)
        return jnp.where(block // tile_blocks == tile_pos, part, jnp.zeros((), BF16))

    keep = block_part(jnp.where(tile_pos == 0, panel_order[0], panel_order[1]))
    send = block_part(jnp.where(tile_pos == 0, panel_order[1], panel_order[0]))
    picked = pick(pair_start[None, :], encoded, keep, lax.ppermute(send, "tile", swap))
    mine = lax.all_gather(picked, "dp", axis=0, tiled=False)
    near = lax.ppermute(mine, "tile", swap)

    by_owner = encoded
    if own_rows != grid_cols:
        by_owner = encoded.reshape(grid_rows, snaps, grid_cols // own_rows, own_rows)
        by_owner = by_owner.transpose(0, 2, 1, 3).reshape(dp_count, snaps, own_rows)
    own_enc = lax.all_to_all(by_owner, "dp", 0, 0, tiled=False)

    low, inv, shift = gram_factor(tile_idx, mine, near, tile_obs * tile_count)
    grow_start = tile_pos * tile_obs + dp_pos * own_rows
    own_block = grow_start // PANEL
    info = jnp.stack(
        [
            tile_pos,
            (own_block == panel_order[0]).astype(jnp.int32),
            (own_block == panel_order[1]).astype(jnp.int32),
            grow_start - own_block * PANEL,
        ]
    ).astype(jnp.int32)
    factor_rows, whitened = whiten_rows(info, starts, own_enc, mine, near, low, inv)
    return (factor_rows[None], whitened[None], shift[0, 0])


def solution(mesh):
    placed = (P("dp", None, "tile", None), P("dp"), P("tile", None), P(), P(), P(), P(), P())
    return jax.shard_map(
        on_device,
        mesh=mesh,
        in_specs=placed,
        out_specs=(P("tile", "dp", None), P("tile", "dp", None), P()),
        check_vma=False,
    )
```

```python
import jax
import jax.numpy as jnp
from jax import lax
from jax.experimental import pallas as pl
from jax.experimental.pallas import tpu as pltpu
from jax.sharding import PartitionSpec as P

F32 = jnp.float32
BF16 = jnp.bfloat16


EDGE = 128
PANEL = 512
HALF = PANEL // 2


def halo_kernel(tile_ref, own_ref, out_ref):
    block = own_ref.shape[0]
    row = lax.broadcasted_iota(jnp.int32, (16, 48), 0)
    col = lax.broadcasted_iota(jnp.int32, (16, 48), 1)
    dist = lax.div(row, 3)
    source = jnp.where(tile_ref[0] == 0, 15 - dist, dist)
    pick = jnp.where((row < 9) & (col == lax.rem(row, 3) * 16 + source), 1.0, 0.0).astype(BF16)
    for base in range(0, block, 3):
        cells = jnp.concatenate(
            [own_ref[base + k].reshape(48, 128) for k in range(3)], axis=1
        )
        rows = jnp.dot(pick, cells, preferred_element_type=F32).astype(BF16)
        for k in range(3):
            out_ref[base + k] = rows[:, 128 * k : 128 * (k + 1)]


def halo_rows(tile_idx, snapshots):
    count = snapshots.shape[0]
    block = next(b for b in (57, 27, 9, 3) if count % b == 0)
    return pl.pallas_call(
        halo_kernel,
        grid=(count // block,),
        in_specs=[
            pl.BlockSpec(memory_space=pltpu.SMEM),
            pl.BlockSpec((block, 3, 16, 128), lambda i: (i, 0, 0, 0)),
        ],
        out_specs=pl.BlockSpec((block, 16, 128), lambda i: (i, 0, 0)),
        out_shape=jax.ShapeDtypeStruct((count, 16, 128), BF16),
        name="halo_rows",
    )(tile_idx, snapshots)


GROUP = 32
BLOCK = 32


def encode_kernel(
    tile_ref, w_ref, gain_ref, bias_ref, readout_ref,
    own_ref, halo_ref, cls_ref, ncls_ref, out_ref,
    mat_ref, gmap_ref, bmap_ref, enc_ref, *, count,
):
    @pl.when(pl.program_id(0) == 0)
    def _():
        tile = tile_ref[0]
        r_out = lax.broadcasted_iota(jnp.int32, (56, 64), 0)
        r_in = lax.broadcasted_iota(jnp.int32, (56, 64), 1)

        def place(r):
            h = r - 48
            outside = jnp.where(tile == 0, 16 + lax.div(h, 3), -1 - lax.div(h, 3))
            return jnp.where(r < 48, lax.div(r, 16), lax.rem(h, 3)), jnp.where(r < 48, lax.rem(r, 16), outside)

        o_idx, o_pos = place(r_out)
        i_idx, i_pos = place(r_in)
        tap = i_pos - o_pos + 1
        good = (tap >= 0) & (tap <= 2) & (r_in < 57) & (r_out < 54)
        code = jnp.where(good, (o_idx * 3 + i_idx) * 3 + tap, -1)
        hits = [code == k for k in range(27)]
        for layer in range(3):
            for b in range(3):
                acc = jnp.zeros((56, 64), F32)
                for k in range(27):
                    weight = w_ref[((layer * 9 + k // 3) * 3 + k % 3) * 3 + b]
                    acc = jnp.where(hits[k], weight, acc)
                high = acc.astype(BF16).astype(F32)
                low = acc - high
                full = jnp.concatenate([high, low, high], axis=1).astype(BF16)
                mat_ref[layer, 56 * b : 56 * (b + 1), :] = full
        own_cls = cls_ref[...]
        near = ncls_ref[...]
        h0 = jnp.where(tile == 0, near[0:1], near[15:16])
        h1 = jnp.where(tile == 0, near[1:2], near[14:15])
        cls = jnp.concatenate([own_cls] * 3 + [h0, h0, h0, h1, h1, h1, h1, h1], axis=0)
        row = lax.broadcasted_iota(jnp.int32, (56, 128), 0)
        field = jnp.where(row < 48, lax.div(row, 16), lax.rem(row - 48, 3))
        for layer in range(3):
            gmap = jnp.zeros((56, 128), F32)
            for c in range(4):
                gmap = jnp.where(cls == c, gain_ref[layer * 4 + c], gmap)
            gmap_ref[layer] = gmap
            bmap = jnp.zeros((56, 128), F32)
            for f in range(3):
                bmap = jnp.where(field == f, bias_ref[layer * 3 + f], bmap)
            bmap_ref[layer] = bmap

    lane = lax.broadcasted_iota(jnp.int32, (56, 128), 1)
    first_lane = lane == 0
    last_lane = lane == 127
    blank = jnp.zeros((8, 128), F32)
    ro = [readout_ref[f] for f in range(3)]

    def group(g, carry):
        base = g * GROUP
        high = []
        low = []
        fields = []
        for k in range(GROUP):
            own = own_ref[base + k].reshape(48, 128)
            halo = halo_ref[base + k]
            high.append(jnp.concatenate([own, halo], axis=0))
            fields.append(
                jnp.concatenate([own.astype(F32), halo.astype(F32)[:8]], axis=0)
            )
        for layer in range(3):
            top = jnp.concatenate(high, axis=1)
            if layer == 0:
                stacked = jnp.concatenate([top, top], axis=0)
                mat = mat_ref[layer, :, 0:128]
            else:
                stacked = jnp.concatenate([top, top, jnp.concatenate(low, axis=1)], axis=0)
                mat = mat_ref[layer]
            sums = jnp.dot(mat, stacked, preferred_element_type=F32)
            high = []
            low = []
            for k in range(GROUP):
                part = sums[:, 128 * k : 128 * (k + 1)]
                left = jnp.where(first_lane, 0.0, pltpu.roll(part[0:56], 1, 1))
                right = jnp.where(last_lane, 0.0, pltpu.roll(part[112:168], 127, 1))
                total = left + part[56:112] + right
                fields[k] = fields[k] + jnp.tanh(gmap_ref[layer] * total + bmap_ref[layer])
                if layer < 2:
                    wide = jnp.concatenate([fields[k], blank], axis=0)
                    upper = wide.astype(BF16)
                    high.append(upper)
                    low.append((wide - upper.astype(F32)).astype(BF16))
        for k in range(GROUP):
            f = fields[k]
            value = ro[0] * f[0:16] + ro[1] * f[16:32] + ro[2] * f[32:48]
            enc_ref[pl.ds((base + k) * 16, 16), :] = value
        return carry

    lax.fori_loop(0, BLOCK // GROUP, group, 0, unroll=True)
    snap = lax.broadcasted_iota(jnp.int32, (BLOCK, 128), 0) + pl.program_id(0) * BLOCK
    for r in range(16):
        rows = enc_ref[pl.ds(r, BLOCK, stride=16), :]
        out_ref[r] = jnp.where(snap < count, rows, 0.0).astype(BF16)


def encode(tile_idx, snapshots, halo, classes, near_classes, stencil_w, depth_gain, bias, readout):
    count = snapshots.shape[0]
    smem = pl.BlockSpec(memory_space=pltpu.SMEM)
    whole = pl.BlockSpec((16, 128), lambda i: (0, 0))

    def body(*refs):
        encode_kernel(*refs, count=count)

    return pl.pallas_call(
        body,
        grid=(pl.cdiv(count, BLOCK),),
        in_specs=[
            smem, smem, smem, smem, smem,
            pl.BlockSpec((BLOCK, 3, 16, 128), lambda i: (i, 0, 0, 0)),
            pl.BlockSpec((BLOCK, 16, 128), lambda i: (i, 0, 0)),
            whole, whole,
        ],
        out_specs=pl.BlockSpec((16, BLOCK, 128), lambda i: (0, i, 0)),
        out_shape=jax.ShapeDtypeStruct((16, pl.cdiv(count, BLOCK) * BLOCK, 128), BF16),
        scratch_shapes=[
            pltpu.VMEM((3, 168, 192), BF16),
            pltpu.VMEM((3, 56, 128), F32),
            pltpu.VMEM((3, 56, 128), F32),
            pltpu.VMEM((BLOCK * 16, 128), F32),
        ],
        name="encode",
    )(
        tile_idx, stencil_w.reshape(-1), depth_gain.reshape(-1), bias.reshape(-1), readout,
        snapshots, halo, classes, near_classes,
    )


def split(x):
    high = x.astype(BF16)
    return high, (x - high.astype(F32)).astype(BF16)


def lhs3(x):
    high, low = split(x)
    return jnp.concatenate([high, high, low], axis=1)


def rhs3(x):
    high, low = split(x)
    return jnp.concatenate([high, low, high], axis=1)


def dot_nt(a, b):
    return lax.dot_general(a, b, (((1,), (1,)), ((), ())), preferred_element_type=F32)


def factor_diag(block, eye):
    row8 = lax.broadcasted_iota(jnp.int32, (8, EDGE), 0)
    groups = EDGE // 8
    a = [block[8 * g : 8 * (g + 1)] for g in range(groups)]
    b = [eye[8 * g : 8 * (g + 1)] for g in range(groups)]

    def lanes(x, j):
        return jnp.broadcast_to(x[:, j : j + 1], (8, EDGE))

    def sublanes(x, i):
        return jnp.broadcast_to(x[i : i + 1, :], (8, EDGE))

    for home in range(groups):
        at = 8 * home
        cols = [lanes(a[home], at + k) for k in range(8)]
        e = [[sublanes(cols[k], i) for k in range(i + 1)] for i in range(8)]
        invert = []
        mult = [[None] * 8 for _ in range(8)]
        for k in range(8):
            invert.append(1.0 / e[k][k])
            for i in range(k + 1, 8):
                mult[i][k] = e[i][k] * invert[k]
            for i in range(k + 1, 8):
                for j in range(k + 1, i + 1):
                    e[i][j] = e[i][j] - mult[i][k] * e[j][k]

        def forward(rows):
            for k in range(8):
                for m in range(k):
                    rows[k] = rows[k] - mult[k][m] * rows[m]
            return rows

        def pack(rows):
            out = rows[0]
            for k in range(1, 8):
                out = jnp.where(row8 == k, rows[k], out)
            return out

        u = forward([sublanes(a[home], k) for k in range(8)])
        v = forward([sublanes(b[home], k) for k in range(8)])
        a[home] = pack(u)
        b[home] = pack(v)
        if home + 1 == groups:
            break
        us = [u[k] * invert[k] for k in range(8)]
        vs = [v[k] * invert[k] for k in range(8)]
        for g in range(home + 1, groups):
            c = forward([lanes(a[g], at + k) for k in range(8)])
            for k in range(8):
                a[g] = a[g] - c[k] * us[k]
                b[g] = b[g] - c[k] * vs[k]
    return jnp.concatenate(a, axis=0), jnp.concatenate(b, axis=0)


def pick_kernel(start_ref, enc_ref, keep_ref, near_ref, top_ref, bottom_ref):
    snaps = enc_ref.shape[1]
    pairs = start_ref.shape[1]
    snap_idx = lax.broadcasted_iota(jnp.int32, (snaps, pairs), 0)
    hit = jnp.where(snap_idx == start_ref[...], 1.0, 0.0).astype(BF16)
    panel = jnp.concatenate(
        [keep_ref[r] + near_ref[r] for r in range(keep_ref.shape[0])], axis=1
    )
    tn = (((0,), (0,)), ((), ()))
    chosen = lax.dot_general(panel, hit, tn, preferred_element_type=F32).astype(BF16)
    top_ref[...] = chosen[0:HALF]
    bottom_ref[0:HALF, :] = chosen[HALF:]
    norms = jnp.zeros(enc_ref.shape[1:], F32)
    for r in range(enc_ref.shape[0]):
        value = enc_ref[r].astype(F32)
        norms = norms + value * value
    total = jnp.zeros((enc_ref.shape[2], pairs), F32)
    for _ in range(3):
        high = norms.astype(BF16)
        total = total + lax.dot_general(high, hit, tn, preferred_element_type=F32)
        norms = norms - high.astype(F32)
    total = jnp.sum(jnp.sum(total, axis=0, keepdims=True), axis=1, keepdims=True)
    rest = jnp.broadcast_to(total, (16, pairs))
    row = lax.broadcasted_iota(jnp.int32, (16, pairs), 0)
    packed = jnp.zeros((16, pairs), BF16)
    for k in range(3):
        high = rest.astype(BF16)
        packed = jnp.where(row == k, high.astype(F32), packed.astype(F32)).astype(BF16)
        rest = rest - high.astype(F32)
    starts = start_ref[...]
    coarse = lax.shift_right_logical(starts, 2)
    for k, value in ((3, coarse), (4, starts - 4 * coarse)):
        packed = jnp.where(row == k, value.astype(F32), packed.astype(F32)).astype(BF16)
    bottom_ref[HALF:, :] = packed


def pick(starts, enc, keep, near):
    pairs = starts.shape[1]
    return pl.pallas_call(
        pick_kernel,
        out_shape=[
            jax.ShapeDtypeStruct((HALF, pairs), BF16),
            jax.ShapeDtypeStruct((HALF + 16, pairs), BF16),
        ],
        compiler_params=pltpu.CompilerParams(vmem_limit_bytes=40 * 2**20),
        name="pick_pairs",
    )(starts, enc, keep, near)


def blocks_of(flip, refs):
    top, bottom, near_top, near_bottom = refs
    mine = jnp.concatenate([top[0], bottom[0, 0:HALF, :]], axis=0)
    near = jnp.concatenate([near_top[0], near_bottom[0, 0:HALF, :]], axis=0)
    return jnp.where(flip, near, mine), jnp.where(flip, mine, near)


def gram_step(tile_ref, pieces, low_ref, power_ref):
    flip = tile_ref[0] == 1
    pairs = [blocks_of(flip, refs) for refs in pieces]
    lead = jnp.concatenate([pair[0] for pair in pairs], axis=1)
    tail = jnp.concatenate([pair[1] for pair in pairs], axis=1)
    low_ref[0:PANEL, 0:PANEL] += dot_nt(lead, lead)
    low_ref[PANEL:, 0:PANEL] += dot_nt(tail, lead)
    low_ref[PANEL:, PANEL:] += dot_nt(tail, tail)
    for refs in pieces:
        for ref in (refs[1], refs[3]):
            part = ref[0, HALF:, 0:EDGE].astype(F32)
            part = part[0:1] + part[1:2] + part[2:3]
            power_ref[...] += jnp.broadcast_to(part, power_ref.shape)


def grouped(refs):
    return [refs[4 * k : 4 * (k + 1)] for k in range(len(refs) // 4)]


def gram_kernel(tile_ref, *refs):
    pieces, (low_ref, power_ref) = refs[:-2], refs[-2:]

    @pl.when(pl.program_id(0) == 0)
    def _():
        low_ref[...] = jnp.zeros(low_ref.shape, F32)
        power_ref[...] = jnp.zeros(power_ref.shape, F32)

    gram_step(tile_ref, grouped(pieces), low_ref, power_ref)


def factor_kernel(tile_ref, sums_ref, energy_ref, *refs, pairs_total, obs):
    pieces, (low_ref, inv_ref, shift_ref) = refs[:-3], refs[-3:]

    @pl.when(pl.program_id(0) == 0)
    def _():
        low_ref[...] = sums_ref[...]
        shift_ref[...] = energy_ref[...]

    gram_step(tile_ref, grouped(pieces), low_ref, shift_ref)

    @pl.when(pl.program_id(0) == pl.num_programs(0) - 1)
    def _():
        shift = 0.5 * (shift_ref[...] / pairs_total) / float(obs)
        shift_ref[...] = shift
        factor(low_ref, inv_ref, shift, 1.0 / pairs_total)


def factor(low_ref, inv_ref, shift, scale):
    width = low_ref.shape[0]
    row = lax.broadcasted_iota(jnp.int32, (EDGE, EDGE), 0)
    col = lax.broadcasted_iota(jnp.int32, (EDGE, EDGE), 1)
    eye = jnp.where(row == col, 1.0, 0.0)
    blocks = width // EDGE
    shift_wide = jnp.concatenate([shift] * (EDGE // 8), axis=0)

    for i in range(blocks):
        rows = pl.ds(EDGE * i, EDGE)
        low_ref[rows, :] = low_ref[rows, :] * scale
        low_ref[rows, EDGE * i : EDGE * (i + 1)] += jnp.where(row == col, shift_wide, 0.0)
        if EDGE * (i + 1) < width:
            low_ref[rows, EDGE * (i + 1) :] = jnp.zeros((EDGE, width - EDGE * (i + 1)), F32)

    def update(k):
        here = EDGE * k
        rest = EDGE * (k + 1)
        below = dot_nt(lhs3(low_ref[rest:, here:rest]), rhs3(inv_ref[here:rest, :]))
        low_ref[rest:, here:rest] = below
        left = lhs3(below)
        right = rhs3(below)
        start = rest
        while start < width:
            stop = start + (2 * EDGE if (width - start) % (2 * EDGE) == 0 else EDGE)
            low_ref[start:, start:stop] -= dot_nt(
                left[start - rest :], right[start - rest : stop - rest]
            )
            start = stop

    def step(k, carry):
        at = pl.ds(pl.multiple_of(k * EDGE, EDGE), EDGE)
        upper, unit = factor_diag(low_ref[at, at], eye)
        pivots = jnp.sum(jnp.where(row == col, upper, 0.0), axis=1, keepdims=True)
        root = lax.rsqrt(pivots)
        low_ref[at, at] = (jnp.where(col >= row, upper, 0.0) * root).T
        inv_ref[at, :] = unit * root
        for static in range(blocks - 1):
            @pl.when(k == static)
            def _():
                update(static)
        return carry

    lax.fori_loop(0, blocks, step, 0)
    for i in range(blocks - 1):
        low_ref[EDGE * i : EDGE * (i + 1), EDGE * (i + 1) : EDGE * (i + 2)] = jnp.zeros((EDGE, EDGE), F32)


def whole(shape):
    return pl.BlockSpec(shape, lambda i: (0,) * len(shape))


def piece_specs(pieces):
    return [pl.BlockSpec((1,) + piece.shape[1:], lambda i: (i, 0, 0)) for piece in pieces]


SUMS = jax.ShapeDtypeStruct((2 * PANEL, 2 * PANEL), F32)
POWER = jax.ShapeDtypeStruct((8, EDGE), F32)
LIMIT = pltpu.CompilerParams(vmem_limit_bytes=56 * 2**20)


def gram_part(tile_idx, pieces):
    return pl.pallas_call(
        gram_kernel,
        grid=(pieces[0].shape[0],),
        in_specs=[pl.BlockSpec(memory_space=pltpu.SMEM)] + piece_specs(pieces),
        out_specs=[whole(SUMS.shape), whole(POWER.shape)],
        out_shape=[SUMS, POWER],
        compiler_params=LIMIT,
        cost_estimate=pl.CostEstimate(
            flops=6 * PANEL**2 * 4 * pieces[0].shape[0] * PANEL,
            transcendentals=0,
            bytes_accessed=sum(2 * x.size for x in pieces) + 4 * SUMS.size,
        ),
        name="gram_part",
    )(tile_idx, *pieces)


def gram_factor(tile_idx, sums, energy, pieces, pairs_total, obs):
    def body(*refs):
        factor_kernel(*refs, pairs_total=pairs_total, obs=obs)

    return pl.pallas_call(
        body,
        grid=(pieces[0].shape[0],),
        in_specs=[pl.BlockSpec(memory_space=pltpu.SMEM), whole(SUMS.shape), whole(POWER.shape)]
        + piece_specs(pieces),
        out_specs=[whole(SUMS.shape), whole((2 * PANEL, EDGE)), whole(POWER.shape)],
        out_shape=[SUMS, jax.ShapeDtypeStruct((2 * PANEL, EDGE), F32), POWER],
        compiler_params=LIMIT,
        name="gram_factor",
    )(tile_idx, sums, energy, *pieces)


def rows_kernel(info_ref, enc_ref, low_ref, inv_ref, *refs, pairs_total):
    pieces, (chol_ref, white_ref, sums_ref) = refs[:-3], refs[-3:]
    step = pl.program_id(0)
    own = chol_ref.shape[0]
    width = 2 * PANEL

    @pl.when(step == 0)
    def _():
        sums_ref[...] = jnp.zeros(sums_ref.shape, F32)

    snaps = enc_ref.shape[1]
    pairs = pieces[0].shape[2]
    snap_idx = lax.broadcasted_iota(jnp.int32, (snaps, pairs), 0)
    tn = (((0,), (0,)), ((), ()))
    flip = info_ref[0] == 1
    top_bit = enc_ref.shape[0] // 2
    parts = grouped(pieces)
    picked = []
    for k in range(len(parts)):
        source = jnp.bitwise_xor(info_ref[4], (k // 4) * top_bit + step * 4 + k % 4)
        values = enc_ref[source]
        packed = parts[k][1][0, HALF:, :].astype(F32)
        starts = (4.0 * packed[3:4] + packed[4:5]).astype(jnp.int32)
        first = jnp.where(snap_idx == starts, 1.0, 0.0).astype(BF16)
        second = jnp.where(snap_idx == starts + 1, 1.0, 0.0).astype(BF16)
        picked.append(
            jnp.concatenate(
                [
                    lax.dot_general(values, first, tn, preferred_element_type=F32),
                    lax.dot_general(values, second, tn, preferred_element_type=F32),
                ],
                axis=0,
            ).astype(BF16)
        )
    both = [blocks_of(flip, part) for part in parts]
    picked = jnp.concatenate(picked, axis=1)
    sums_ref[:, 0:PANEL] += dot_nt(picked, jnp.concatenate([b[0] for b in both], axis=1))
    sums_ref[:, PANEL:] += dot_nt(picked, jnp.concatenate([b[1] for b in both], axis=1))

    @pl.when(step == pl.num_programs(0) - 1)
    def _():
        sums_ref[...] = sums_ref[...] * (1.0 / pairs_total)
        for k in range(width // EDGE):
            here = EDGE * k
            rest = EDGE * (k + 1)
            solved = dot_nt(lhs3(sums_ref[:, here:rest]), rhs3(inv_ref[here:rest, :]))
            sums_ref[:, here:rest] = solved
            if rest < width:
                sums_ref[:, rest:] -= dot_nt(lhs3(solved), rhs3(low_ref[rest:, here:rest]))
        offset = info_ref[3]
        first_rows = low_ref[pl.ds(pl.multiple_of(offset, 8), own), :]
        second_rows = low_ref[pl.ds(pl.multiple_of(PANEL + offset, 8), own), :]
        chol_ref[...] = jnp.where(
            info_ref[1] == 1,
            first_rows,
            jnp.where(info_ref[2] == 1, second_rows, sums_ref[0:own, :]),
        )
        white_ref[...] = sums_ref[own:, :]


def whiten_rows(info, enc, low, inv, pieces, pairs_total):
    own = enc.shape[2]
    width = 2 * PANEL

    def body(*refs):
        rows_kernel(*refs, pairs_total=pairs_total)

    return pl.pallas_call(
        body,
        grid=(pieces[0].shape[0],),
        in_specs=[pl.BlockSpec(memory_space=pltpu.SMEM)]
        + [whole(x.shape) for x in (enc, low, inv)]
        + piece_specs(pieces),
        out_specs=[whole((own, width))] * 2,
        out_shape=[jax.ShapeDtypeStruct((own, width), F32)] * 2,
        scratch_shapes=[pltpu.VMEM((2 * own, width), F32)],
        compiler_params=LIMIT,
        name="whiten_rows",
    )(info, enc, low, inv, *pieces)


def after_kernel(value_ref, *refs):
    del value_ref, refs


def after(value, *earlier):
    hbm = pl.BlockSpec(memory_space=pl.ANY)
    return pl.pallas_call(
        after_kernel,
        in_specs=[hbm] * (1 + len(earlier)),
        out_specs=hbm,
        out_shape=jax.ShapeDtypeStruct(value.shape, value.dtype),
        input_output_aliases={0: 0},
        name="after",
    )(value, *earlier)


def gather_pieces(parts, dp_count, swap, tile_idx):
    def across(arrays, bit):
        pairs = [(i, i ^ bit) for i in range(dp_count)]
        return [lax.ppermute(x, "dp", pairs) for x in arrays]

    top_bit = dp_count // 2
    chunks = []
    sums = None
    for start in (parts, across(parts, top_bit)):
        bit = 4
        while bit < top_bit:
            far = across(start, bit)
            start = [jnp.concatenate(pair, axis=0) for pair in zip(start, far)]
            bit *= 2
        top, bottom = start
        (top_x,) = across([top], 1)
        (bottom_y,) = across([bottom], 2)
        (top_y,) = across([top], 2)
        (bottom_x,) = across([bottom], 1)
        (top_xy,) = across([top_x], 2)
        (bottom_xy,) = across([bottom_y], 1)
        if sums is not None:
            top_xy = after(top_xy, *sums)
        pieces = []
        for pair in ((top, bottom), (top_x, bottom_x), (top_y, bottom_y), (top_xy, bottom_xy)):
            pieces.extend(pair)
            pieces.extend(lax.ppermute(x, "tile", swap) for x in pair)
        chunks.append(pieces)
        if sums is None:
            sums = gram_part(tile_idx, pieces)
    return chunks, sums


def on_device(
    snapshots, pair_start, bath_class, stencil_w, depth_gain, stencil_bias, readout, panel_order
):
    tile_pos = lax.axis_index("tile")
    dp_pos = lax.axis_index("dp")
    tile_count = lax.axis_size("tile")
    dp_count = lax.axis_size("dp")
    grid_rows, grid_cols = bath_class.shape
    tile_obs = grid_rows * grid_cols
    own_rows = tile_obs // dp_count
    swap = [(0, 1), (1, 0)]
    tile_idx = tile_pos[None].astype(jnp.int32)

    near_class = lax.ppermute(bath_class, "tile", swap)
    halo = lax.ppermute(halo_rows(tile_idx, snapshots), "tile", swap)
    encoded = encode(
        tile_idx, snapshots, halo, bath_class, near_class,
        stencil_w, depth_gain, stencil_bias, readout,
    )
    snaps = encoded.shape[1]

    block_rows = PANEL // grid_cols
    tile_blocks = tile_obs // PANEL

    def block_part(block):
        at = (block % tile_blocks) * block_rows
        part = lax.dynamic_slice_in_dim(encoded, at, block_rows, 0)
        return jnp.where(block // tile_blocks == tile_pos, part, jnp.zeros((), BF16))

    keep = block_part(jnp.where(tile_pos == 0, panel_order[0], panel_order[1]))
    send = block_part(jnp.where(tile_pos == 0, panel_order[1], panel_order[0]))
    own_parts = pick(pair_start[None, :], encoded, keep, lax.ppermute(send, "tile", swap))
    chunks, sums = gather_pieces([part[None] for part in own_parts], dp_count, swap, tile_idx)

    by_owner = encoded
    if own_rows != grid_cols:
        by_owner = encoded.reshape(grid_rows, snaps, grid_cols // own_rows, own_rows)
        by_owner = by_owner.transpose(0, 2, 1, 3).reshape(dp_count, snaps, own_rows)
    by_owner = after(by_owner, *chunks[0], *chunks[1])
    own_enc = lax.all_to_all(by_owner, "dp", 0, 0, tiled=False)

    pairs_total = float(pair_start.shape[0] * dp_count)
    low, inv, shift = gram_factor(
        tile_idx, *sums, chunks[1], pairs_total, tile_obs * tile_count
    )
    grow_start = tile_pos * tile_obs + dp_pos * own_rows
    own_block = grow_start // PANEL
    info = jnp.stack(
        [
            tile_pos,
            (own_block == panel_order[0]).astype(jnp.int32),
            (own_block == panel_order[1]).astype(jnp.int32),
            grow_start - own_block * PANEL,
            dp_pos,
        ]
    ).astype(jnp.int32)
    factor_rows, whitened = whiten_rows(
        info, own_enc, low, inv, chunks[0] + chunks[1], pairs_total
    )
    return (factor_rows[None], whitened[None], shift[0, 0])


def solution(mesh):
    placed = (P("dp", None, "tile", None), P("dp"), P("tile", None), P(), P(), P(), P(), P())
    return jax.shard_map(
        on_device,
        mesh=mesh,
        in_specs=placed,
        out_specs=(P("tile", "dp", None), P("tile", "dp", None), P()),
        check_vma=False,
    )
```

```python
import jax
import jax.numpy as jnp
from jax import lax
from jax.experimental import pallas as pl
from jax.experimental.pallas import tpu as pltpu
from jax.sharding import PartitionSpec as P

F32 = jnp.float32
BF16 = jnp.bfloat16


EDGE = 128
PANEL = 512
HALF = PANEL // 2


def halo_kernel(tile_ref, own_ref, out_ref):
    block = own_ref.shape[0]
    row = lax.broadcasted_iota(jnp.int32, (16, 24), 0)
    col = lax.broadcasted_iota(jnp.int32, (16, 24), 1)
    dist = lax.div(row, 3)
    source = jnp.where(tile_ref[0] == 0, 7 - dist, dist)
    pick = jnp.where((row < 9) & (col == lax.rem(row, 3) * 8 + source), 1.0, 0.0).astype(BF16)
    group = block // 3
    for base in range(0, block, group):
        cells = jnp.concatenate(
            [own_ref[base + k].astype(F32).reshape(24, 128) for k in range(group)], axis=1
        ).astype(BF16)
        rows = jnp.dot(pick, cells, preferred_element_type=F32).astype(BF16)
        for k in range(group):
            out_ref[base + k] = rows[:, 128 * k : 128 * (k + 1)]


def halo_rows(tile_idx, snapshots):
    count = snapshots.shape[0]
    block = next(b for b in (57, 27, 9, 3) if count % b == 0)
    return pl.pallas_call(
        halo_kernel,
        grid_spec=pltpu.PrefetchScalarGridSpec(
            num_scalar_prefetch=1,
            grid=(count // block,),
            in_specs=[pl.BlockSpec((block, 3, 8, 128), lambda i, tile: (i, 0, 1 - tile[0], 0))],
            out_specs=pl.BlockSpec((block, 16, 128), lambda i, tile: (i, 0, 0)),
        ),
        out_shape=jax.ShapeDtypeStruct((count, 16, 128), BF16),
        name="halo_rows",
    )(tile_idx, snapshots)


GROUP = 48
BLOCK = 48


def encode_kernel(
    tile_ref, w_ref, gain_ref, bias_ref, readout_ref,
    own_ref, halo_ref, cls_ref, ncls_ref, out_ref,
    mat_ref, gmap_ref, bmap_ref, enc_ref, *, count,
):
    @pl.when(pl.program_id(0) == 0)
    def _():
        tile = tile_ref[0]
        r_out = lax.broadcasted_iota(jnp.int32, (56, 64), 0)
        r_in = lax.broadcasted_iota(jnp.int32, (56, 64), 1)

        def place(r):
            h = r - 48
            outside = jnp.where(tile == 0, 16 + lax.div(h, 3), -1 - lax.div(h, 3))
            return jnp.where(r < 48, lax.div(r, 16), lax.rem(h, 3)), jnp.where(r < 48, lax.rem(r, 16), outside)

        o_idx, o_pos = place(r_out)
        i_idx, i_pos = place(r_in)
        tap = i_pos - o_pos + 1
        good = (tap >= 0) & (tap <= 2) & (r_in < 57) & (r_out < 54)
        code = jnp.where(good, (o_idx * 3 + i_idx) * 3 + tap, -1)
        hits = [code == k for k in range(27)]
        for layer in range(3):
            for b in range(3):
                acc = jnp.zeros((56, 64), F32)
                for k in range(27):
                    weight = w_ref[((layer * 9 + k // 3) * 3 + k % 3) * 3 + b]
                    acc = jnp.where(hits[k], weight, acc)
                high = acc.astype(BF16).astype(F32)
                low = acc - high
                full = jnp.concatenate([high, low, high], axis=1).astype(BF16)
                mat_ref[layer, 56 * b : 56 * (b + 1), :] = full
        own_cls = cls_ref[...]
        near = ncls_ref[...]
        h0 = jnp.where(tile == 0, near[0:1], near[15:16])
        h1 = jnp.where(tile == 0, near[1:2], near[14:15])
        cls = jnp.concatenate([own_cls] * 3 + [h0, h0, h0, h1, h1, h1, h1, h1], axis=0)
        row = lax.broadcasted_iota(jnp.int32, (56, 128), 0)
        field = jnp.where(row < 48, lax.div(row, 16), lax.rem(row - 48, 3))
        for layer in range(3):
            gmap = jnp.zeros((56, 128), F32)
            for c in range(4):
                gmap = jnp.where(cls == c, gain_ref[layer * 4 + c], gmap)
            gmap_ref[layer] = gmap
            bmap = jnp.zeros((56, 128), F32)
            for f in range(3):
                bmap = jnp.where(field == f, bias_ref[layer * 3 + f], bmap)
            bmap_ref[layer] = bmap

    lane = lax.broadcasted_iota(jnp.int32, (56, 128), 1)
    first_lane = lane == 0
    last_lane = lane == 127
    blank = jnp.zeros((8, 128), F32)
    ro = [readout_ref[f] for f in range(3)]

    def group(g, carry):
        base = g * GROUP
        high = []
        low = []
        fields = []
        for k in range(GROUP):
            own = own_ref[base + k].reshape(48, 128)
            halo = halo_ref[base + k]
            high.append(jnp.concatenate([own, halo], axis=0))
            fields.append(
                jnp.concatenate([own.astype(F32), halo.astype(F32)[:8]], axis=0)
            )
        for layer in range(3):
            top = jnp.concatenate(high, axis=1)
            if layer == 0:
                stacked = jnp.concatenate([top, top], axis=0)
                mat = mat_ref[layer, :, 0:128]
            else:
                stacked = jnp.concatenate([top, top, jnp.concatenate(low, axis=1)], axis=0)
                mat = mat_ref[layer]
            sums = jnp.dot(mat, stacked, preferred_element_type=F32)
            high = []
            low = []
            for k in range(GROUP):
                part = sums[:, 128 * k : 128 * (k + 1)]
                left = jnp.where(first_lane, 0.0, pltpu.roll(part[0:56], 1, 1))
                right = jnp.where(last_lane, 0.0, pltpu.roll(part[112:168], 127, 1))
                total = left + part[56:112] + right
                fields[k] = fields[k] + jnp.tanh(gmap_ref[layer] * total + bmap_ref[layer])
                if layer < 2:
                    wide = jnp.concatenate([fields[k], blank], axis=0)
                    upper = wide.astype(BF16)
                    high.append(upper)
                    low.append((wide - upper.astype(F32)).astype(BF16))
        for k in range(GROUP):
            f = fields[k]
            value = ro[0] * f[0:16] + ro[1] * f[16:32] + ro[2] * f[32:48]
            enc_ref[pl.ds((base + k) * 16, 16), :] = value
        return carry

    lax.fori_loop(0, BLOCK // GROUP, group, 0, unroll=True)
    snap = lax.broadcasted_iota(jnp.int32, (BLOCK, 128), 0) + pl.program_id(0) * BLOCK
    for r in range(16):
        rows = enc_ref[pl.ds(r, BLOCK, stride=16), :]
        out_ref[r] = jnp.where(snap < count, rows, 0.0).astype(BF16)


def encode(tile_idx, snapshots, halo, classes, near_classes, stencil_w, depth_gain, bias, readout):
    count = snapshots.shape[0]
    smem = pl.BlockSpec(memory_space=pltpu.SMEM)
    whole = pl.BlockSpec((16, 128), lambda i: (0, 0))

    def body(*refs):
        encode_kernel(*refs, count=count)

    return pl.pallas_call(
        body,
        grid=(pl.cdiv(count, BLOCK),),
        in_specs=[
            smem, smem, smem, smem, smem,
            pl.BlockSpec((BLOCK, 3, 16, 128), lambda i: (i, 0, 0, 0)),
            pl.BlockSpec((BLOCK, 16, 128), lambda i: (i, 0, 0)),
            whole, whole,
        ],
        out_specs=pl.BlockSpec((16, BLOCK, 128), lambda i: (0, i, 0)),
        out_shape=jax.ShapeDtypeStruct((16, pl.cdiv(count, BLOCK) * BLOCK, 128), BF16),
        scratch_shapes=[
            pltpu.VMEM((3, 168, 192), BF16),
            pltpu.VMEM((3, 56, 128), F32),
            pltpu.VMEM((3, 56, 128), F32),
            pltpu.VMEM((BLOCK * 16, 128), F32),
        ],
        name="encode",
    )(
        tile_idx, stencil_w.reshape(-1), depth_gain.reshape(-1), bias.reshape(-1), readout,
        snapshots, halo, classes, near_classes,
    )


def split(x):
    high = x.astype(BF16)
    return high, (x - high.astype(F32)).astype(BF16)


def lhs3(x):
    high, low = split(x)
    return jnp.concatenate([high, high, low], axis=1)


def rhs3(x):
    high, low = split(x)
    return jnp.concatenate([high, low, high], axis=1)


def dot_nt(a, b):
    return lax.dot_general(a, b, (((1,), (1,)), ((), ())), preferred_element_type=F32)


def factor_diag(block, eye):
    row8 = lax.broadcasted_iota(jnp.int32, (8, EDGE), 0)
    groups = EDGE // 8
    a = [block[8 * g : 8 * (g + 1)] for g in range(groups)]
    b = [eye[8 * g : 8 * (g + 1)] for g in range(groups)]

    def lanes(x, j):
        return jnp.broadcast_to(x[:, j : j + 1], (8, EDGE))

    def sublanes(x, i):
        return jnp.broadcast_to(x[i : i + 1, :], (8, EDGE))

    for home in range(groups):
        at = 8 * home
        cols = [lanes(a[home], at + k) for k in range(8)]
        e = [[sublanes(cols[k], i) for k in range(i + 1)] for i in range(8)]
        root = []
        mult = [[None] * 8 for _ in range(8)]
        for k in range(8):
            root.append(lax.rsqrt(e[k][k]))
            for i in range(k + 1, 8):
                mult[i][k] = e[i][k] * root[k]
            for i in range(k + 1, 8):
                for j in range(k + 1, i + 1):
                    e[i][j] = e[i][j] - mult[i][k] * mult[j][k]

        def forward(rows):
            for k in range(8):
                for m in range(k):
                    rows[k] = rows[k] - mult[k][m] * rows[m]
                rows[k] = rows[k] * root[k]
            return rows

        def pack(rows):
            out = rows[0]
            for k in range(1, 8):
                out = jnp.where(row8 == k, rows[k], out)
            return out

        u = forward([sublanes(a[home], k) for k in range(8)])
        v = forward([sublanes(b[home], k) for k in range(8)])
        a[home] = pack(u)
        b[home] = pack(v)
        for g in range(home + 1, groups):
            c = forward([lanes(a[g], at + k) for k in range(8)])
            for k in range(8):
                a[g] = a[g] - c[k] * u[k]
                b[g] = b[g] - c[k] * v[k]
    return jnp.concatenate(a, axis=0), jnp.concatenate(b, axis=0)


def pick_kernel(start_ref, enc_ref, keep_ref, near_ref, top_ref, bottom_ref):
    snaps = enc_ref.shape[1]
    pairs = start_ref.shape[1]
    snap_idx = lax.broadcasted_iota(jnp.int32, (snaps, pairs), 0)
    hit = jnp.where(snap_idx == start_ref[...], 1.0, 0.0).astype(BF16)
    panel = jnp.concatenate(
        [keep_ref[r] + near_ref[r] for r in range(keep_ref.shape[0])], axis=1
    )
    tn = (((0,), (0,)), ((), ()))
    chosen = lax.dot_general(panel, hit, tn, preferred_element_type=F32).astype(BF16)
    top_ref[...] = chosen[0:HALF]
    bottom_ref[0:HALF, :] = chosen[HALF:]
    norms = jnp.zeros(enc_ref.shape[1:], F32)
    for r in range(enc_ref.shape[0]):
        value = enc_ref[r].astype(F32)
        norms = norms + value * value
    total = jnp.zeros((enc_ref.shape[2], pairs), F32)
    for _ in range(3):
        high = norms.astype(BF16)
        total = total + lax.dot_general(high, hit, tn, preferred_element_type=F32)
        norms = norms - high.astype(F32)
    total = jnp.sum(jnp.sum(total, axis=0, keepdims=True), axis=1, keepdims=True)
    rest = jnp.broadcast_to(total, (16, pairs))
    row = lax.broadcasted_iota(jnp.int32, (16, pairs), 0)
    packed = jnp.zeros((16, pairs), BF16)
    for k in range(3):
        high = rest.astype(BF16)
        packed = jnp.where(row == k, high.astype(F32), packed.astype(F32)).astype(BF16)
        rest = rest - high.astype(F32)
    starts = start_ref[...]
    coarse = lax.shift_right_logical(starts, 2)
    for k, value in ((3, coarse), (4, starts - 4 * coarse)):
        packed = jnp.where(row == k, value.astype(F32), packed.astype(F32)).astype(BF16)
    bottom_ref[HALF:, :] = packed


def pick(starts, enc, keep, near):
    pairs = starts.shape[1]
    return pl.pallas_call(
        pick_kernel,
        out_shape=[
            jax.ShapeDtypeStruct((HALF, pairs), BF16),
            jax.ShapeDtypeStruct((HALF + 16, pairs), BF16),
        ],
        compiler_params=pltpu.CompilerParams(vmem_limit_bytes=40 * 2**20),
        name="pick_pairs",
    )(starts, enc, keep, near)


def blocks_of(flip, refs):
    top, bottom, near_top, near_bottom = refs
    mine = jnp.concatenate([top[0], bottom[0, 0:HALF, :]], axis=0)
    near = jnp.concatenate([near_top[0], near_bottom[0, 0:HALF, :]], axis=0)
    return jnp.where(flip, near, mine), jnp.where(flip, mine, near)


def gram_step(tile_ref, pieces, low_ref, power_ref):
    flip = tile_ref[0] == 1
    pairs = [blocks_of(flip, refs) for refs in pieces]
    lead = jnp.concatenate([pair[0] for pair in pairs], axis=1)
    tail = jnp.concatenate([pair[1] for pair in pairs], axis=1)
    low_ref[PANEL:, 0:PANEL] += dot_nt(tail, lead)
    for base, part in ((0, lead), (PANEL, tail)):
        low_ref[base : base + PANEL, base : base + HALF] += dot_nt(part, part[0:HALF])
        low_ref[base + HALF : base + PANEL, base + HALF : base + PANEL] += dot_nt(
            part[HALF:], part[HALF:]
        )
    for refs in pieces:
        for ref in (refs[1], refs[3]):
            part = ref[0, HALF:, 0:EDGE].astype(F32)
            part = part[0:1] + part[1:2] + part[2:3]
            power_ref[...] += jnp.broadcast_to(part, power_ref.shape)


def grouped(refs):
    return [refs[4 * k : 4 * (k + 1)] for k in range(len(refs) // 4)]


def gram_kernel(tile_ref, *refs):
    pieces, (low_ref, power_ref) = refs[:-2], refs[-2:]

    @pl.when(pl.program_id(0) == 0)
    def _():
        low_ref[...] = jnp.zeros(low_ref.shape, F32)
        power_ref[...] = jnp.zeros(power_ref.shape, F32)

    gram_step(tile_ref, grouped(pieces), low_ref, power_ref)


def factor_kernel(tile_ref, sums_ref, energy_ref, *refs, pairs_total, obs):
    pieces, (low_ref, inv_ref, shift_ref) = refs[:-3], refs[-3:]

    @pl.when(pl.program_id(0) == 0)
    def _():
        low_ref[...] = sums_ref[...]
        shift_ref[...] = energy_ref[...]

    gram_step(tile_ref, grouped(pieces), low_ref, shift_ref)

    @pl.when(pl.program_id(0) == pl.num_programs(0) - 1)
    def _():
        shift = 0.5 * (shift_ref[...] / pairs_total) / float(obs)
        shift_ref[...] = shift
        factor(low_ref, inv_ref, shift, 1.0 / pairs_total)


def factor(low_ref, inv_ref, shift, scale):
    width = low_ref.shape[0]
    row = lax.broadcasted_iota(jnp.int32, (EDGE, EDGE), 0)
    col = lax.broadcasted_iota(jnp.int32, (EDGE, EDGE), 1)
    eye = jnp.where(row == col, 1.0, 0.0)
    blocks = width // EDGE
    shift_wide = jnp.concatenate([shift] * (EDGE // 8), axis=0)

    for i in range(blocks):
        rows = pl.ds(EDGE * i, EDGE)
        low_ref[rows, :] = low_ref[rows, :] * scale
        low_ref[rows, EDGE * i : EDGE * (i + 1)] += jnp.where(row == col, shift_wide, 0.0)
        if EDGE * (i + 1) < width:
            low_ref[rows, EDGE * (i + 1) :] = jnp.zeros((EDGE, width - EDGE * (i + 1)), F32)

    def update(k):
        here = EDGE * k
        rest = EDGE * (k + 1)
        below = dot_nt(lhs3(low_ref[rest:, here:rest]), rhs3(inv_ref[here:rest, :]))
        low_ref[rest:, here:rest] = below
        left = lhs3(below)
        right = rhs3(below)
        start = rest
        while start < width:
            stop = start + (2 * EDGE if (width - start) % (2 * EDGE) == 0 else EDGE)
            low_ref[start:, start:stop] -= dot_nt(
                left[start - rest :], right[start - rest : stop - rest]
            )
            start = stop

    def step(k, carry):
        at = pl.ds(pl.multiple_of(k * EDGE, EDGE), EDGE)
        upper, inverse = factor_diag(low_ref[at, at], eye)
        low_ref[at, at] = jnp.where(col >= row, upper, 0.0).T
        inv_ref[at, :] = inverse
        for static in range(blocks - 1):
            @pl.when(k == static)
            def _():
                update(static)
        return carry

    lax.fori_loop(0, blocks, step, 0)
    for i in range(blocks - 1):
        low_ref[EDGE * i : EDGE * (i + 1), EDGE * (i + 1) : EDGE * (i + 2)] = jnp.zeros((EDGE, EDGE), F32)


def whole(shape):
    return pl.BlockSpec(shape, lambda i: (0,) * len(shape))


def piece_specs(pieces):
    return [pl.BlockSpec((1,) + piece.shape[1:], lambda i: (i, 0, 0)) for piece in pieces]


SUMS = jax.ShapeDtypeStruct((2 * PANEL, 2 * PANEL), F32)
POWER = jax.ShapeDtypeStruct((8, EDGE), F32)
LIMIT = pltpu.CompilerParams(vmem_limit_bytes=56 * 2**20)


def gram_part(tile_idx, pieces):
    return pl.pallas_call(
        gram_kernel,
        grid=(pieces[0].shape[0],),
        in_specs=[pl.BlockSpec(memory_space=pltpu.SMEM)] + piece_specs(pieces),
        out_specs=[whole(SUMS.shape), whole(POWER.shape)],
        out_shape=[SUMS, POWER],
        compiler_params=LIMIT,
        cost_estimate=pl.CostEstimate(
            flops=6 * PANEL**2 * 4 * pieces[0].shape[0] * PANEL,
            transcendentals=0,
            bytes_accessed=sum(2 * x.size for x in pieces) + 4 * SUMS.size,
        ),
        name="gram_part",
    )(tile_idx, *pieces)


def gram_factor(tile_idx, sums, energy, pieces, pairs_total, obs):
    def body(*refs):
        factor_kernel(*refs, pairs_total=pairs_total, obs=obs)

    return pl.pallas_call(
        body,
        grid=(pieces[0].shape[0],),
        in_specs=[pl.BlockSpec(memory_space=pltpu.SMEM), whole(SUMS.shape), whole(POWER.shape)]
        + piece_specs(pieces),
        out_specs=[whole(SUMS.shape), whole((2 * PANEL, EDGE)), whole(POWER.shape)],
        out_shape=[SUMS, jax.ShapeDtypeStruct((2 * PANEL, EDGE), F32), POWER],
        compiler_params=LIMIT,
        name="gram_factor",
    )(tile_idx, sums, energy, *pieces)


def rows_kernel(info_ref, enc_ref, low_ref, inv_ref, *refs, pairs_total):
    pieces, (chol_ref, white_ref, sums_ref) = refs[:-3], refs[-3:]
    step = pl.program_id(0)
    own = chol_ref.shape[0]
    width = 2 * PANEL

    @pl.when(step == 0)
    def _():
        sums_ref[...] = jnp.zeros(sums_ref.shape, F32)

    snaps = enc_ref.shape[1]
    pairs = pieces[0].shape[2]
    snap_idx = lax.broadcasted_iota(jnp.int32, (snaps, pairs), 0)
    tn = (((0,), (0,)), ((), ()))
    flip = info_ref[0] == 1
    top_bit = enc_ref.shape[0] // 2
    parts = grouped(pieces)
    picked = []
    for k in range(len(parts)):
        source = jnp.bitwise_xor(info_ref[4], (k // 4) * top_bit + step * 4 + k % 4)
        values = enc_ref[source]
        packed = parts[k][1][0, HALF:, :].astype(F32)
        starts = (4.0 * packed[3:4] + packed[4:5]).astype(jnp.int32)
        hit = jnp.where(snap_idx == starts, 1.0, 0.0).astype(BF16)
        following = pltpu.roll(values.astype(F32), snaps - 1, 0).astype(BF16)
        if own % EDGE == 0:
            wide = jnp.concatenate([values, following], axis=1)
            rows = lax.dot_general(wide, hit, tn, preferred_element_type=F32)
        else:
            rows = jnp.concatenate(
                [
                    lax.dot_general(values, hit, tn, preferred_element_type=F32),
                    lax.dot_general(following, hit, tn, preferred_element_type=F32),
                ],
                axis=0,
            )
        picked.append(rows.astype(BF16))
    both = [blocks_of(flip, part) for part in parts]
    picked = jnp.concatenate(picked, axis=1)
    sums_ref[:, 0:PANEL] += dot_nt(picked, jnp.concatenate([b[0] for b in both], axis=1))
    sums_ref[:, PANEL:] += dot_nt(picked, jnp.concatenate([b[1] for b in both], axis=1))

    @pl.when(step == pl.num_programs(0) - 1)
    def _():
        sums_ref[...] = sums_ref[...] * (1.0 / pairs_total)
        for k in range(width // EDGE):
            here = EDGE * k
            rest = EDGE * (k + 1)
            solved = dot_nt(lhs3(sums_ref[:, here:rest]), rhs3(inv_ref[here:rest, :]))
            sums_ref[:, here:rest] = solved
            if rest < width:
                sums_ref[:, rest:] -= dot_nt(lhs3(solved), rhs3(low_ref[rest:, here:rest]))
        offset = info_ref[3]
        first_rows = low_ref[pl.ds(pl.multiple_of(offset, 8), own), :]
        second_rows = low_ref[pl.ds(pl.multiple_of(PANEL + offset, 8), own), :]
        chol_ref[...] = jnp.where(
            info_ref[1] == 1,
            first_rows,
            jnp.where(info_ref[2] == 1, second_rows, sums_ref[0:own, :]),
        )
        white_ref[...] = sums_ref[own:, :]


def whiten_rows(info, enc, low, inv, pieces, pairs_total):
    own = enc.shape[2]
    width = 2 * PANEL

    def body(*refs):
        rows_kernel(*refs, pairs_total=pairs_total)

    return pl.pallas_call(
        body,
        grid=(pieces[0].shape[0],),
        in_specs=[pl.BlockSpec(memory_space=pltpu.SMEM)]
        + [whole(x.shape) for x in (enc, low, inv)]
        + piece_specs(pieces),
        out_specs=[whole((own, width))] * 2,
        out_shape=[jax.ShapeDtypeStruct((own, width), F32)] * 2,
        scratch_shapes=[pltpu.VMEM((2 * own, width), F32)],
        compiler_params=LIMIT,
        name="whiten_rows",
    )(info, enc, low, inv, *pieces)


def after_kernel(value_ref, *refs):
    del value_ref, refs


def after(value, *earlier):
    hbm = pl.BlockSpec(memory_space=pl.ANY)
    return pl.pallas_call(
        after_kernel,
        in_specs=[hbm] * (1 + len(earlier)),
        out_specs=hbm,
        out_shape=jax.ShapeDtypeStruct(value.shape, value.dtype),
        input_output_aliases={0: 0},
        name="after",
    )(value, *earlier)


def gather_pieces(parts, dp_count, swap, tile_idx):
    def across(arrays, bit):
        pairs = [(i, i ^ bit) for i in range(dp_count)]
        return [lax.ppermute(x, "dp", pairs) for x in arrays]

    top_bit = dp_count // 2
    chunks = []
    sums = None
    for start in (parts, across(parts, top_bit)):
        bit = 4
        while bit < top_bit:
            far = across(start, bit)
            start = [jnp.concatenate(pair, axis=0) for pair in zip(start, far)]
            bit *= 2
        top, bottom = start
        (top_x,) = across([top], 1)
        (bottom_y,) = across([bottom], 2)
        (top_y,) = across([top], 2)
        (bottom_x,) = across([bottom], 1)
        (top_xy,) = across([top_x], 2)
        (bottom_xy,) = across([bottom_y], 1)
        if sums is not None:
            top_xy = after(top_xy, *sums)
        pieces = []
        for pair in ((top, bottom), (top_x, bottom_x), (top_y, bottom_y), (top_xy, bottom_xy)):
            pieces.extend(pair)
            pieces.extend(lax.ppermute(x, "tile", swap) for x in pair)
        chunks.append(pieces)
        if sums is None:
            sums = gram_part(tile_idx, pieces)
    return chunks, sums


def on_device(
    snapshots, pair_start, bath_class, stencil_w, depth_gain, stencil_bias, readout, panel_order
):
    tile_pos = lax.axis_index("tile")
    dp_pos = lax.axis_index("dp")
    tile_count = lax.axis_size("tile")
    dp_count = lax.axis_size("dp")
    grid_rows, grid_cols = bath_class.shape
    tile_obs = grid_rows * grid_cols
    own_rows = tile_obs // dp_count
    swap = [(0, 1), (1, 0)]
    tile_idx = tile_pos[None].astype(jnp.int32)

    near_class = lax.ppermute(bath_class, "tile", swap)
    halo = lax.ppermute(halo_rows(tile_idx, snapshots), "tile", swap)
    encoded = encode(
        tile_idx, snapshots, halo, bath_class, near_class,
        stencil_w, depth_gain, stencil_bias, readout,
    )
    snaps = encoded.shape[1]

    block_rows = PANEL // grid_cols
    tile_blocks = tile_obs // PANEL

    def block_part(block):
        at = (block % tile_blocks) * block_rows
        part = lax.dynamic_slice_in_dim(encoded, at, block_rows, 0)
        return jnp.where(block // tile_blocks == tile_pos, part, jnp.zeros((), BF16))

    keep = block_part(jnp.where(tile_pos == 0, panel_order[0], panel_order[1]))
    send = block_part(jnp.where(tile_pos == 0, panel_order[1], panel_order[0]))
    own_parts = pick(pair_start[None, :], encoded, keep, lax.ppermute(send, "tile", swap))
    chunks, sums = gather_pieces([part[None] for part in own_parts], dp_count, swap, tile_idx)

    by_owner = encoded
    if own_rows != grid_cols:
        by_owner = encoded.reshape(grid_rows, snaps, grid_cols // own_rows, own_rows)
        by_owner = by_owner.transpose(0, 2, 1, 3).reshape(dp_count, snaps, own_rows)
    by_owner = after(by_owner, *chunks[0], *chunks[1])
    own_enc = lax.all_to_all(by_owner, "dp", 0, 0, tiled=False)

    pairs_total = float(pair_start.shape[0] * dp_count)
    low, inv, shift = gram_factor(
        tile_idx, *sums, chunks[1], pairs_total, tile_obs * tile_count
    )
    grow_start = tile_pos * tile_obs + dp_pos * own_rows
    own_block = grow_start // PANEL
    info = jnp.stack(
        [
            tile_pos,
            (own_block == panel_order[0]).astype(jnp.int32),
            (own_block == panel_order[1]).astype(jnp.int32),
            grow_start - own_block * PANEL,
            dp_pos,
        ]
    ).astype(jnp.int32)
    factor_rows, whitened = whiten_rows(
        info, own_enc, low, inv, chunks[0] + chunks[1], pairs_total
    )
    return (factor_rows[None], whitened[None], shift[0, 0])


def solution(mesh):
    placed = (P("dp", None, "tile", None), P("dp"), P("tile", None), P(), P(), P(), P(), P())
    return jax.shard_map(
        on_device,
        mesh=mesh,
        in_specs=placed,
        out_specs=(P("tile", "dp", None), P("tile", "dp", None), P()),
        check_vma=False,
    )
```

```python
import jax
import jax.numpy as jnp
from jax import lax
from jax.experimental import pallas as pl
from jax.experimental.pallas import tpu as pltpu
from jax.sharding import PartitionSpec as P

F32 = jnp.float32
BF16 = jnp.bfloat16


EDGE = 128
PANEL = 512
HALF = PANEL // 2


def halo_kernel(tile_ref, own_ref, out_ref):
    block = own_ref.shape[0]
    row = lax.broadcasted_iota(jnp.int32, (16, 24), 0)
    col = lax.broadcasted_iota(jnp.int32, (16, 24), 1)
    dist = lax.div(row, 3)
    source = jnp.where(tile_ref[0] == 0, 7 - dist, dist)
    pick = jnp.where((row < 9) & (col == lax.rem(row, 3) * 8 + source), 1.0, 0.0).astype(BF16)
    group = block // 3
    for base in range(0, block, group):
        cells = jnp.concatenate(
            [own_ref[base + k].astype(F32).reshape(24, 128) for k in range(group)], axis=1
        ).astype(BF16)
        rows = jnp.dot(pick, cells, preferred_element_type=F32).astype(BF16)
        for k in range(group):
            out_ref[base + k] = rows[:, 128 * k : 128 * (k + 1)]


def halo_rows(tile_idx, snapshots):
    count = snapshots.shape[0]
    block = next(b for b in (57, 27, 9, 3) if count % b == 0)
    return pl.pallas_call(
        halo_kernel,
        grid_spec=pltpu.PrefetchScalarGridSpec(
            num_scalar_prefetch=1,
            grid=(count // block,),
            in_specs=[pl.BlockSpec((block, 3, 8, 128), lambda i, tile: (i, 0, 1 - tile[0], 0))],
            out_specs=pl.BlockSpec((block, 16, 128), lambda i, tile: (i, 0, 0)),
        ),
        out_shape=jax.ShapeDtypeStruct((count, 16, 128), BF16),
        name="halo_rows",
    )(tile_idx, snapshots)


GROUP = 48
BLOCK = 48


def encode_kernel(
    tile_ref, w_ref, gain_ref, bias_ref, readout_ref,
    own_ref, halo_ref, cls_ref, ncls_ref, out_ref,
    mat_ref, gmap_ref, bmap_ref, enc_ref, *, count,
):
    @pl.when(pl.program_id(0) == 0)
    def _():
        tile = tile_ref[0]
        r_out = lax.broadcasted_iota(jnp.int32, (56, 64), 0)
        r_in = lax.broadcasted_iota(jnp.int32, (56, 64), 1)

        def place(r):
            h = r - 48
            outside = jnp.where(tile == 0, 16 + lax.div(h, 3), -1 - lax.div(h, 3))
            return jnp.where(r < 48, lax.div(r, 16), lax.rem(h, 3)), jnp.where(r < 48, lax.rem(r, 16), outside)

        o_idx, o_pos = place(r_out)
        i_idx, i_pos = place(r_in)
        tap = i_pos - o_pos + 1
        good = (tap >= 0) & (tap <= 2) & (r_in < 57) & (r_out < 54)
        code = jnp.where(good, (o_idx * 3 + i_idx) * 3 + tap, -1)
        hits = [code == k for k in range(27)]
        for layer in range(3):
            for b in range(3):
                acc = jnp.zeros((56, 64), F32)
                for k in range(27):
                    weight = w_ref[((layer * 9 + k // 3) * 3 + k % 3) * 3 + b]
                    acc = jnp.where(hits[k], weight, acc)
                high = acc.astype(BF16).astype(F32)
                low = acc - high
                full = jnp.concatenate([high, low, high], axis=1).astype(BF16)
                mat_ref[layer, 56 * b : 56 * (b + 1), :] = full
        own_cls = cls_ref[...]
        near = ncls_ref[...]
        h0 = jnp.where(tile == 0, near[0:1], near[15:16])
        h1 = jnp.where(tile == 0, near[1:2], near[14:15])
        cls = jnp.concatenate([own_cls] * 3 + [h0, h0, h0, h1, h1, h1, h1, h1], axis=0)
        row = lax.broadcasted_iota(jnp.int32, (56, 128), 0)
        field = jnp.where(row < 48, lax.div(row, 16), lax.rem(row - 48, 3))
        for layer in range(3):
            gmap = jnp.zeros((56, 128), F32)
            for c in range(4):
                gmap = jnp.where(cls == c, gain_ref[layer * 4 + c], gmap)
            gmap_ref[layer] = gmap
            bmap = jnp.zeros((56, 128), F32)
            for f in range(3):
                bmap = jnp.where(field == f, bias_ref[layer * 3 + f], bmap)
            bmap_ref[layer] = bmap

    lane = lax.broadcasted_iota(jnp.int32, (56, 128), 1)
    first_lane = lane == 0
    last_lane = lane == 127
    blank = jnp.zeros((8, 128), F32)
    ro = [readout_ref[f] for f in range(3)]

    def group(g, carry):
        base = g * GROUP
        high = []
        low = []
        fields = []
        for k in range(GROUP):
            own = own_ref[base + k].reshape(48, 128)
            halo = halo_ref[base + k]
            high.append(jnp.concatenate([own, halo], axis=0))
            fields.append(
                jnp.concatenate([own.astype(F32), halo.astype(F32)[:8]], axis=0)
            )
        for layer in range(3):
            top = jnp.concatenate(high, axis=1)
            if layer == 0:
                stacked = jnp.concatenate([top, top], axis=0)
                mat = mat_ref[layer, :, 0:128]
            else:
                stacked = jnp.concatenate([top, top, jnp.concatenate(low, axis=1)], axis=0)
                mat = mat_ref[layer]
            sums = jnp.dot(mat, stacked, preferred_element_type=F32)
            high = []
            low = []
            for k in range(GROUP):
                part = sums[:, 128 * k : 128 * (k + 1)]
                left = jnp.where(first_lane, 0.0, pltpu.roll(part[0:56], 1, 1))
                right = jnp.where(last_lane, 0.0, pltpu.roll(part[112:168], 127, 1))
                total = left + part[56:112] + right
                fields[k] = fields[k] + jnp.tanh(gmap_ref[layer] * total + bmap_ref[layer])
                if layer < 2:
                    wide = jnp.concatenate([fields[k], blank], axis=0)
                    upper = wide.astype(BF16)
                    high.append(upper)
                    low.append((wide - upper.astype(F32)).astype(BF16))
        for k in range(GROUP):
            f = fields[k]
            value = ro[0] * f[0:16] + ro[1] * f[16:32] + ro[2] * f[32:48]
            enc_ref[pl.ds((base + k) * 16, 16), :] = value
        return carry

    lax.fori_loop(0, BLOCK // GROUP, group, 0, unroll=True)
    snap = lax.broadcasted_iota(jnp.int32, (BLOCK, 128), 0) + pl.program_id(0) * BLOCK
    for r in range(16):
        rows = enc_ref[pl.ds(r, BLOCK, stride=16), :]
        out_ref[r] = jnp.where(snap < count, rows, 0.0).astype(BF16)


def encode(tile_idx, snapshots, halo, classes, near_classes, stencil_w, depth_gain, bias, readout):
    count = snapshots.shape[0]
    smem = pl.BlockSpec(memory_space=pltpu.SMEM)
    whole = pl.BlockSpec((16, 128), lambda i: (0, 0))

    def body(*refs):
        encode_kernel(*refs, count=count)

    return pl.pallas_call(
        body,
        grid=(pl.cdiv(count, BLOCK),),
        in_specs=[
            smem, smem, smem, smem, smem,
            pl.BlockSpec((BLOCK, 3, 16, 128), lambda i: (i, 0, 0, 0)),
            pl.BlockSpec((BLOCK, 16, 128), lambda i: (i, 0, 0)),
            whole, whole,
        ],
        out_specs=pl.BlockSpec((16, BLOCK, 128), lambda i: (0, i, 0)),
        out_shape=jax.ShapeDtypeStruct((16, pl.cdiv(count, BLOCK) * BLOCK, 128), BF16),
        scratch_shapes=[
            pltpu.VMEM((3, 168, 192), BF16),
            pltpu.VMEM((3, 56, 128), F32),
            pltpu.VMEM((3, 56, 128), F32),
            pltpu.VMEM((BLOCK * 16, 128), F32),
        ],
        name="encode",
    )(
        tile_idx, stencil_w.reshape(-1), depth_gain.reshape(-1), bias.reshape(-1), readout,
        snapshots, halo, classes, near_classes,
    )


def split(x):
    high = x.astype(BF16)
    return high, (x - high.astype(F32)).astype(BF16)


def lhs3(x):
    high, low = split(x)
    return jnp.concatenate([high, high, low], axis=1)


def rhs3(x):
    high, low = split(x)
    return jnp.concatenate([high, low, high], axis=1)


def dot_nt(a, b):
    return lax.dot_general(a, b, (((1,), (1,)), ((), ())), preferred_element_type=F32)


def factor_diag(block, eye):
    row8 = lax.broadcasted_iota(jnp.int32, (8, EDGE), 0)
    groups = EDGE // 8
    a = [block[8 * g : 8 * (g + 1)] for g in range(groups)]
    b = [eye[8 * g : 8 * (g + 1)] for g in range(groups)]

    def lanes(x, j):
        return jnp.broadcast_to(x[:, j : j + 1], (8, EDGE))

    def sublanes(x, i):
        return jnp.broadcast_to(x[i : i + 1, :], (8, EDGE))

    for home in range(groups):
        at = 8 * home
        cols = [lanes(a[home], at + k) for k in range(8)]
        e = [[sublanes(cols[k], i) for k in range(i + 1)] for i in range(8)]
        root = []
        mult = [[None] * 8 for _ in range(8)]
        for k in range(8):
            root.append(lax.rsqrt(e[k][k]))
            for i in range(k + 1, 8):
                mult[i][k] = e[i][k] * root[k]
            for i in range(k + 1, 8):
                for j in range(k + 1, i + 1):
                    e[i][j] = e[i][j] - mult[i][k] * mult[j][k]

        def forward(rows):
            for k in range(8):
                for m in range(k):
                    rows[k] = rows[k] - mult[k][m] * rows[m]
                rows[k] = rows[k] * root[k]
            return rows

        def pack(rows):
            out = rows[0]
            for k in range(1, 8):
                out = jnp.where(row8 == k, rows[k], out)
            return out

        u = forward([sublanes(a[home], k) for k in range(8)])
        v = forward([sublanes(b[home], k) for k in range(8)])
        a[home] = pack(u)
        b[home] = pack(v)
        for g in range(home + 1, groups):
            c = forward([lanes(a[g], at + k) for k in range(8)])
            for k in range(8):
                a[g] = a[g] - c[k] * u[k]
                b[g] = b[g] - c[k] * v[k]
    return jnp.concatenate(a, axis=0), jnp.concatenate(b, axis=0)


def pick_kernel(start_ref, enc_ref, keep_ref, near_ref, top_ref, bottom_ref):
    snaps = enc_ref.shape[1]
    pairs = start_ref.shape[1]
    snap_idx = lax.broadcasted_iota(jnp.int32, (snaps, pairs), 0)
    hit = jnp.where(snap_idx == start_ref[...], 1.0, 0.0).astype(BF16)
    panel = jnp.concatenate(
        [keep_ref[r] + near_ref[r] for r in range(keep_ref.shape[0])], axis=1
    )
    tn = (((0,), (0,)), ((), ()))
    chosen = lax.dot_general(panel, hit, tn, preferred_element_type=F32).astype(BF16)
    top_ref[...] = chosen[0:HALF]
    bottom_ref[0:HALF, :] = chosen[HALF:]
    norms = jnp.zeros(enc_ref.shape[1:], F32)
    for r in range(enc_ref.shape[0]):
        value = enc_ref[r].astype(F32)
        norms = norms + value * value
    total = jnp.zeros((enc_ref.shape[2], pairs), F32)
    for _ in range(3):
        high = norms.astype(BF16)
        total = total + lax.dot_general(high, hit, tn, preferred_element_type=F32)
        norms = norms - high.astype(F32)
    total = jnp.sum(jnp.sum(total, axis=0, keepdims=True), axis=1, keepdims=True)
    rest = jnp.broadcast_to(total, (16, pairs))
    row = lax.broadcasted_iota(jnp.int32, (16, pairs), 0)
    packed = jnp.zeros((16, pairs), BF16)
    for k in range(3):
        high = rest.astype(BF16)
        packed = jnp.where(row == k, high.astype(F32), packed.astype(F32)).astype(BF16)
        rest = rest - high.astype(F32)
    starts = start_ref[...]
    coarse = lax.shift_right_logical(starts, 2)
    for k, value in ((3, coarse), (4, starts - 4 * coarse)):
        packed = jnp.where(row == k, value.astype(F32), packed.astype(F32)).astype(BF16)
    bottom_ref[HALF:, :] = packed


def pick(starts, enc, keep, near):
    pairs = starts.shape[1]
    return pl.pallas_call(
        pick_kernel,
        out_shape=[
            jax.ShapeDtypeStruct((HALF, pairs), BF16),
            jax.ShapeDtypeStruct((HALF + 16, pairs), BF16),
        ],
        compiler_params=pltpu.CompilerParams(vmem_limit_bytes=40 * 2**20),
        name="pick_pairs",
    )(starts, enc, keep, near)


def blocks_of(flip, refs):
    top, bottom, near_top, near_bottom = refs
    mine = jnp.concatenate([top[0], bottom[0, 0:HALF, :]], axis=0)
    near = jnp.concatenate([near_top[0], near_bottom[0, 0:HALF, :]], axis=0)
    return jnp.where(flip, near, mine), jnp.where(flip, mine, near)


def gram_step(tile_ref, pieces, low_ref, power_ref):
    flip = tile_ref[0] == 1
    pairs = [blocks_of(flip, refs) for refs in pieces]
    lead = jnp.concatenate([pair[0] for pair in pairs], axis=1)
    tail = jnp.concatenate([pair[1] for pair in pairs], axis=1)
    low_ref[PANEL:, 0:PANEL] += dot_nt(tail, lead)
    for base, part in ((0, lead), (PANEL, tail)):
        low_ref[base : base + PANEL, base : base + HALF] += dot_nt(part, part[0:HALF])
        low_ref[base + HALF : base + PANEL, base + HALF : base + PANEL] += dot_nt(
            part[HALF:], part[HALF:]
        )

    @pl.when(pl.program_id(1) == 0)
    def _():
        for refs in pieces:
            for ref in (refs[1], refs[3]):
                part = ref[0, HALF:, 0:EDGE].astype(F32)
                part = part[0:1] + part[1:2] + part[2:3]
                power_ref[...] += jnp.broadcast_to(part, power_ref.shape)


def grouped(refs):
    return [refs[4 * k : 4 * (k + 1)] for k in range(len(refs) // 4)]


def gram_kernel(tile_ref, *refs):
    pieces, (low_ref, power_ref) = refs[:-2], refs[-2:]

    @pl.when(at_step(0, 0))
    def _():
        low_ref[...] = jnp.zeros(low_ref.shape, F32)
        power_ref[...] = jnp.zeros(power_ref.shape, F32)

    gram_step(tile_ref, grouped(pieces), low_ref, power_ref)


def factor_kernel(tile_ref, sums_ref, energy_ref, *refs, pairs_total, obs):
    pieces, (low_ref, inv_ref, out_ref, shift_ref) = refs[:-4], refs[-4:]

    @pl.when(at_step(0, 0))
    def _():
        low_ref[...] = sums_ref[...]
        shift_ref[...] = energy_ref[...]

    gram_step(tile_ref, grouped(pieces), low_ref, shift_ref)

    @pl.when(at_step(pl.num_programs(0) - 1, SPLIT - 1))
    def _():
        shift = 0.5 * (shift_ref[...] / pairs_total) / float(obs)
        out_ref[0, 0] = shift[0, 0]
        factor(low_ref, inv_ref, shift, 1.0 / pairs_total)


def factor(low_ref, inv_ref, shift, scale):
    width = low_ref.shape[0]
    row = lax.broadcasted_iota(jnp.int32, (EDGE, EDGE), 0)
    col = lax.broadcasted_iota(jnp.int32, (EDGE, EDGE), 1)
    eye = jnp.where(row == col, 1.0, 0.0)
    blocks = width // EDGE
    shift_wide = jnp.concatenate([shift] * (EDGE // 8), axis=0)

    for i in range(blocks):
        rows = pl.ds(EDGE * i, EDGE)
        low_ref[rows, :] = low_ref[rows, :] * scale
        low_ref[rows, EDGE * i : EDGE * (i + 1)] += jnp.where(row == col, shift_wide, 0.0)
        if EDGE * (i + 1) < width:
            low_ref[rows, EDGE * (i + 1) :] = jnp.zeros((EDGE, width - EDGE * (i + 1)), F32)

    def update(k):
        here = EDGE * k
        rest = EDGE * (k + 1)
        below = dot_nt(lhs3(low_ref[rest:, here:rest]), rhs3(inv_ref[here:rest, :]))
        low_ref[rest:, here:rest] = below
        left = lhs3(below)
        right = rhs3(below)
        start = rest
        while start < width:
            stop = start + (2 * EDGE if (width - start) % (2 * EDGE) == 0 else EDGE)
            low_ref[start:, start:stop] -= dot_nt(
                left[start - rest :], right[start - rest : stop - rest]
            )
            start = stop

    def step(k, carry):
        at = pl.ds(pl.multiple_of(k * EDGE, EDGE), EDGE)
        upper, inverse = factor_diag(low_ref[at, at], eye)
        low_ref[at, at] = jnp.where(col >= row, upper, 0.0).T
        inv_ref[at, :] = inverse
        for static in range(blocks - 1):
            @pl.when(k == static)
            def _():
                update(static)
        return carry

    lax.fori_loop(0, blocks, step, 0)
    for i in range(blocks - 1):
        low_ref[EDGE * i : EDGE * (i + 1), EDGE * (i + 1) : EDGE * (i + 2)] = jnp.zeros((EDGE, EDGE), F32)


SPLIT = 2


def whole(shape):
    return pl.BlockSpec(shape, lambda i, j: (0,) * len(shape))


def piece_specs(pieces):
    return [
        pl.BlockSpec((1, piece.shape[1], piece.shape[2] // SPLIT), lambda i, j: (i, 0, j))
        for piece in pieces
    ]


def at_step(i, j):
    return (pl.program_id(0) == i) & (pl.program_id(1) == j)


SUMS = jax.ShapeDtypeStruct((2 * PANEL, 2 * PANEL), F32)
POWER = jax.ShapeDtypeStruct((8, EDGE), F32)
LIMIT = pltpu.CompilerParams(vmem_limit_bytes=56 * 2**20)


def gram_part(tile_idx, pieces):
    return pl.pallas_call(
        gram_kernel,
        grid=(pieces[0].shape[0], SPLIT),
        in_specs=[pl.BlockSpec(memory_space=pltpu.SMEM)] + piece_specs(pieces),
        out_specs=[whole(SUMS.shape), whole(POWER.shape)],
        out_shape=[SUMS, POWER],
        compiler_params=LIMIT,
        cost_estimate=pl.CostEstimate(
            flops=6 * PANEL**2 * 4 * pieces[0].shape[0] * PANEL,
            transcendentals=0,
            bytes_accessed=sum(2 * x.size for x in pieces) + 4 * SUMS.size,
        ),
        name="gram_part",
    )(tile_idx, *pieces)


def gram_factor(tile_idx, sums, energy, pieces, pairs_total, obs):
    def body(*refs):
        factor_kernel(*refs, pairs_total=pairs_total, obs=obs)

    return pl.pallas_call(
        body,
        grid=(pieces[0].shape[0], SPLIT),
        in_specs=[pl.BlockSpec(memory_space=pltpu.SMEM), whole(SUMS.shape), whole(POWER.shape)]
        + piece_specs(pieces),
        out_specs=[
            whole(SUMS.shape),
            whole((2 * PANEL, EDGE)),
            pl.BlockSpec(memory_space=pltpu.SMEM),
        ],
        out_shape=[
            SUMS,
            jax.ShapeDtypeStruct((2 * PANEL, EDGE), F32),
            jax.ShapeDtypeStruct((1, 1), F32),
        ],
        scratch_shapes=[pltpu.VMEM(POWER.shape, F32)],
        compiler_params=LIMIT,
        name="gram_factor",
    )(tile_idx, sums, energy, *pieces)


def rows_kernel(info_ref, enc_ref, low_ref, inv_ref, *refs, pairs_total):
    pieces, (chol_ref, white_ref, sums_ref) = refs[:-3], refs[-3:]
    step = pl.program_id(0)
    own = chol_ref.shape[0]
    width = 2 * PANEL

    @pl.when(at_step(0, 0))
    def _():
        sums_ref[...] = jnp.zeros(sums_ref.shape, F32)

    snaps = enc_ref.shape[1]
    pairs = pieces[0].shape[2]
    snap_idx = lax.broadcasted_iota(jnp.int32, (snaps, pairs), 0)
    tn = (((0,), (0,)), ((), ()))
    flip = info_ref[0] == 1
    top_bit = enc_ref.shape[0] // 2
    parts = grouped(pieces)
    picked = []
    for k in range(len(parts)):
        source = jnp.bitwise_xor(info_ref[4], (k // 4) * top_bit + step * 4 + k % 4)
        values = enc_ref[source]
        packed = parts[k][1][0, HALF:, :].astype(F32)
        starts = (4.0 * packed[3:4] + packed[4:5]).astype(jnp.int32)
        hit = jnp.where(snap_idx == starts, 1.0, 0.0).astype(BF16)
        following = pltpu.roll(values.astype(F32), snaps - 1, 0).astype(BF16)
        if own % EDGE == 0:
            wide = jnp.concatenate([values, following], axis=1)
            rows = lax.dot_general(wide, hit, tn, preferred_element_type=F32)
        else:
            rows = jnp.concatenate(
                [
                    lax.dot_general(values, hit, tn, preferred_element_type=F32),
                    lax.dot_general(following, hit, tn, preferred_element_type=F32),
                ],
                axis=0,
            )
        picked.append(rows.astype(BF16))
    both = [blocks_of(flip, part) for part in parts]
    picked = jnp.concatenate(picked, axis=1)
    sums_ref[:, 0:PANEL] += dot_nt(picked, jnp.concatenate([b[0] for b in both], axis=1))
    sums_ref[:, PANEL:] += dot_nt(picked, jnp.concatenate([b[1] for b in both], axis=1))

    @pl.when(at_step(pl.num_programs(0) - 1, SPLIT - 1))
    def _():
        sums_ref[...] = sums_ref[...] * (1.0 / pairs_total)
        for k in range(width // EDGE):
            here = EDGE * k
            rest = EDGE * (k + 1)
            solved = dot_nt(lhs3(sums_ref[:, here:rest]), rhs3(inv_ref[here:rest, :]))
            sums_ref[:, here:rest] = solved
            if rest < width:
                sums_ref[:, rest:] -= dot_nt(lhs3(solved), rhs3(low_ref[rest:, here:rest]))
        offset = info_ref[3]
        first_rows = low_ref[pl.ds(pl.multiple_of(offset, 8), own), :]
        second_rows = low_ref[pl.ds(pl.multiple_of(PANEL + offset, 8), own), :]
        chol_ref[...] = jnp.where(
            info_ref[1] == 1,
            first_rows,
            jnp.where(info_ref[2] == 1, second_rows, sums_ref[0:own, :]),
        )
        white_ref[...] = sums_ref[own:, :]


def whiten_rows(info, enc, low, inv, pieces, pairs_total):
    own = enc.shape[2]
    width = 2 * PANEL

    def body(*refs):
        rows_kernel(*refs, pairs_total=pairs_total)

    return pl.pallas_call(
        body,
        grid=(pieces[0].shape[0], SPLIT),
        in_specs=[pl.BlockSpec(memory_space=pltpu.SMEM)]
        + [whole(x.shape) for x in (enc, low, inv)]
        + piece_specs(pieces),
        out_specs=[whole((own, width))] * 2,
        out_shape=[jax.ShapeDtypeStruct((own, width), F32)] * 2,
        scratch_shapes=[pltpu.VMEM((2 * own, width), F32)],
        compiler_params=LIMIT,
        name="whiten_rows",
    )(info, enc, low, inv, *pieces)


def after_kernel(value_ref, *refs):
    del value_ref, refs


def after(value, *earlier):
    hbm = pl.BlockSpec(memory_space=pl.ANY)
    return pl.pallas_call(
        after_kernel,
        in_specs=[hbm] * (1 + len(earlier)),
        out_specs=hbm,
        out_shape=jax.ShapeDtypeStruct(value.shape, value.dtype),
        input_output_aliases={0: 0},
        name="after",
    )(value, *earlier)


def gather_pieces(parts, dp_count, swap, tile_idx):
    def across(arrays, bit):
        pairs = [(i, i ^ bit) for i in range(dp_count)]
        return [lax.ppermute(x, "dp", pairs) for x in arrays]

    top_bit = dp_count // 2
    chunks = []
    sums = None
    for start in (parts, across(parts, top_bit)):
        bit = 4
        while bit < top_bit:
            far = across(start, bit)
            start = [jnp.concatenate(pair, axis=0) for pair in zip(start, far)]
            bit *= 2
        top, bottom = start
        (top_x,) = across([top], 1)
        (bottom_y,) = across([bottom], 2)
        (top_y,) = across([top], 2)
        (bottom_x,) = across([bottom], 1)
        (top_xy,) = across([top_x], 2)
        (bottom_xy,) = across([bottom_y], 1)
        if sums is not None:
            top_xy = after(top_xy, *sums)
        pieces = []
        for pair in ((top, bottom), (top_x, bottom_x), (top_y, bottom_y), (top_xy, bottom_xy)):
            pieces.extend(pair)
            pieces.extend(lax.ppermute(x, "tile", swap) for x in pair)
        chunks.append(pieces)
        if sums is None:
            sums = gram_part(tile_idx, pieces)
    return chunks, sums


def on_device(
    snapshots, pair_start, bath_class, stencil_w, depth_gain, stencil_bias, readout, panel_order
):
    tile_pos = lax.axis_index("tile")
    dp_pos = lax.axis_index("dp")
    tile_count = lax.axis_size("tile")
    dp_count = lax.axis_size("dp")
    grid_rows, grid_cols = bath_class.shape
    tile_obs = grid_rows * grid_cols
    own_rows = tile_obs // dp_count
    swap = [(0, 1), (1, 0)]
    tile_idx = tile_pos[None].astype(jnp.int32)

    near_class = lax.ppermute(bath_class, "tile", swap)
    halo = lax.ppermute(halo_rows(tile_idx, snapshots), "tile", swap)
    encoded = encode(
        tile_idx, snapshots, halo, bath_class, near_class,
        stencil_w, depth_gain, stencil_bias, readout,
    )
    snaps = encoded.shape[1]

    block_rows = PANEL // grid_cols
    tile_blocks = tile_obs // PANEL

    def block_part(block):
        at = (block % tile_blocks) * block_rows
        part = lax.dynamic_slice_in_dim(encoded, at, block_rows, 0)
        return jnp.where(block // tile_blocks == tile_pos, part, jnp.zeros((), BF16))

    keep = block_part(jnp.where(tile_pos == 0, panel_order[0], panel_order[1]))
    send = block_part(jnp.where(tile_pos == 0, panel_order[1], panel_order[0]))
    own_parts = pick(pair_start[None, :], encoded, keep, lax.ppermute(send, "tile", swap))
    chunks, sums = gather_pieces([part[None] for part in own_parts], dp_count, swap, tile_idx)

    by_owner = encoded
    if own_rows != grid_cols:
        by_owner = encoded.reshape(grid_rows, snaps, grid_cols // own_rows, own_rows)
        by_owner = by_owner.transpose(0, 2, 1, 3).reshape(dp_count, snaps, own_rows)
    by_owner = after(by_owner, *chunks[0], *chunks[1])
    own_enc = lax.all_to_all(by_owner, "dp", 0, 0, tiled=False)

    pairs_total = float(pair_start.shape[0] * dp_count)
    low, inv, shift = gram_factor(
        tile_idx, *sums, chunks[1], pairs_total, tile_obs * tile_count
    )
    grow_start = tile_pos * tile_obs + dp_pos * own_rows
    own_block = grow_start // PANEL
    info = jnp.stack(
        [
            tile_pos,
            (own_block == panel_order[0]).astype(jnp.int32),
            (own_block == panel_order[1]).astype(jnp.int32),
            grow_start - own_block * PANEL,
            dp_pos,
        ]
    ).astype(jnp.int32)
    factor_rows, whitened = whiten_rows(
        info, own_enc, low, inv, chunks[0] + chunks[1], pairs_total
    )
    return (factor_rows[None], whitened[None], shift.reshape(()))


def solution(mesh):
    placed = (P("dp", None, "tile", None), P("dp"), P("tile", None), P(), P(), P(), P(), P())
    return jax.shard_map(
        on_device,
        mesh=mesh,
        in_specs=placed,
        out_specs=(P("tile", "dp", None), P("tile", "dp", None), P()),
        check_vma=False,
    )
```

```python
import jax
import jax.numpy as jnp
from jax import lax
from jax.experimental import pallas as pl
from jax.experimental.pallas import tpu as pltpu
from jax.sharding import PartitionSpec as P

F32 = jnp.float32
BF16 = jnp.bfloat16


EDGE = 128
PANEL = 512
HALF = PANEL // 2


def halo_kernel(tile_ref, own_ref, out_ref):
    block = own_ref.shape[0]
    row = lax.broadcasted_iota(jnp.int32, (16, 24), 0)
    col = lax.broadcasted_iota(jnp.int32, (16, 24), 1)
    dist = lax.div(row, 3)
    source = jnp.where(tile_ref[0] == 0, 7 - dist, dist)
    pick = jnp.where((row < 9) & (col == lax.rem(row, 3) * 8 + source), 1.0, 0.0).astype(BF16)
    group = block // 3
    for base in range(0, block, group):
        cells = jnp.concatenate(
            [own_ref[base + k].astype(F32).reshape(24, 128) for k in range(group)], axis=1
        ).astype(BF16)
        rows = jnp.dot(pick, cells, preferred_element_type=F32).astype(BF16)
        for k in range(group):
            out_ref[base + k] = rows[:, 128 * k : 128 * (k + 1)]


def halo_rows(tile_idx, snapshots):
    count = snapshots.shape[0]
    block = next(b for b in (57, 27, 9, 3) if count % b == 0)
    return pl.pallas_call(
        halo_kernel,
        grid_spec=pltpu.PrefetchScalarGridSpec(
            num_scalar_prefetch=1,
            grid=(count // block,),
            in_specs=[pl.BlockSpec((block, 3, 8, 128), lambda i, tile: (i, 0, 1 - tile[0], 0))],
            out_specs=pl.BlockSpec((block, 16, 128), lambda i, tile: (i, 0, 0)),
        ),
        out_shape=jax.ShapeDtypeStruct((count, 16, 128), BF16),
        name="halo_rows",
    )(tile_idx, snapshots)


GROUP = 48
BLOCK = 48


def encode_kernel(
    tile_ref, w_ref, gain_ref, bias_ref, readout_ref,
    own_ref, halo_ref, cls_ref, ncls_ref, out_ref,
    mat_ref, gmap_ref, bmap_ref, enc_ref, *, count,
):
    @pl.when(pl.program_id(0) == 0)
    def _():
        tile = tile_ref[0]
        r_out = lax.broadcasted_iota(jnp.int32, (56, 64), 0)
        r_in = lax.broadcasted_iota(jnp.int32, (56, 64), 1)

        def place(r):
            h = r - 48
            outside = jnp.where(tile == 0, 16 + lax.div(h, 3), -1 - lax.div(h, 3))
            return jnp.where(r < 48, lax.div(r, 16), lax.rem(h, 3)), jnp.where(r < 48, lax.rem(r, 16), outside)

        o_idx, o_pos = place(r_out)
        i_idx, i_pos = place(r_in)
        tap = i_pos - o_pos + 1
        good = (tap >= 0) & (tap <= 2) & (r_in < 57) & (r_out < 54)
        code = jnp.where(good, (o_idx * 3 + i_idx) * 3 + tap, -1)
        hits = [code == k for k in range(27)]
        for layer in range(3):
            for b in range(3):
                acc = jnp.zeros((56, 64), F32)
                for k in range(27):
                    weight = w_ref[((layer * 9 + k // 3) * 3 + k % 3) * 3 + b]
                    acc = jnp.where(hits[k], weight, acc)
                high = acc.astype(BF16).astype(F32)
                low = acc - high
                full = jnp.concatenate([high, low, high], axis=1).astype(BF16)
                mat_ref[layer, 56 * b : 56 * (b + 1), :] = full
        own_cls = cls_ref[...]
        near = ncls_ref[...]
        h0 = jnp.where(tile == 0, near[0:1], near[15:16])
        h1 = jnp.where(tile == 0, near[1:2], near[14:15])
        cls = jnp.concatenate([own_cls] * 3 + [h0, h0, h0, h1, h1, h1, h1, h1], axis=0)
        row = lax.broadcasted_iota(jnp.int32, (56, 128), 0)
        field = jnp.where(row < 48, lax.div(row, 16), lax.rem(row - 48, 3))
        for layer in range(3):
            gmap = jnp.zeros((56, 128), F32)
            for c in range(4):
                gmap = jnp.where(cls == c, gain_ref[layer * 4 + c], gmap)
            gmap_ref[layer] = gmap
            bmap = jnp.zeros((56, 128), F32)
            for f in range(3):
                bmap = jnp.where(field == f, bias_ref[layer * 3 + f], bmap)
            bmap_ref[layer] = bmap

    lane = lax.broadcasted_iota(jnp.int32, (56, 128), 1)
    first_lane = lane == 0
    last_lane = lane == 127
    blank = jnp.zeros((8, 128), F32)
    ro = [readout_ref[f] for f in range(3)]

    def group(g, carry):
        base = g * GROUP
        high = []
        low = []
        fields = []
        for k in range(GROUP):
            own = own_ref[base + k].reshape(48, 128)
            halo = halo_ref[base + k]
            high.append(jnp.concatenate([own, halo], axis=0))
            fields.append(
                jnp.concatenate([own.astype(F32), halo.astype(F32)[:8]], axis=0)
            )
        for layer in range(3):
            top = jnp.concatenate(high, axis=1)
            if layer == 0:
                stacked = jnp.concatenate([top, top], axis=0)
                mat = mat_ref[layer, :, 0:128]
            else:
                stacked = jnp.concatenate([top, top, jnp.concatenate(low, axis=1)], axis=0)
                mat = mat_ref[layer]
            sums = jnp.dot(mat, stacked, preferred_element_type=F32)
            high = []
            low = []
            for k in range(GROUP):
                part = sums[:, 128 * k : 128 * (k + 1)]
                left = jnp.where(first_lane, 0.0, pltpu.roll(part[0:56], 1, 1))
                right = jnp.where(last_lane, 0.0, pltpu.roll(part[112:168], 127, 1))
                total = left + part[56:112] + right
                fields[k] = fields[k] + jnp.tanh(gmap_ref[layer] * total + bmap_ref[layer])
                if layer < 2:
                    wide = jnp.concatenate([fields[k], blank], axis=0)
                    upper = wide.astype(BF16)
                    high.append(upper)
                    low.append((wide - upper.astype(F32)).astype(BF16))
        for k in range(GROUP):
            f = fields[k]
            value = ro[0] * f[0:16] + ro[1] * f[16:32] + ro[2] * f[32:48]
            enc_ref[pl.ds((base + k) * 16, 16), :] = value
        return carry

    lax.fori_loop(0, BLOCK // GROUP, group, 0, unroll=True)
    snap = lax.broadcasted_iota(jnp.int32, (BLOCK, 128), 0) + pl.program_id(0) * BLOCK
    for r in range(16):
        rows = enc_ref[pl.ds(r, BLOCK, stride=16), :]
        out_ref[r] = jnp.where(snap < count, rows, 0.0).astype(BF16)


def encode(tile_idx, snapshots, halo, classes, near_classes, stencil_w, depth_gain, bias, readout):
    count = snapshots.shape[0]
    smem = pl.BlockSpec(memory_space=pltpu.SMEM)
    whole = pl.BlockSpec((16, 128), lambda i: (0, 0))

    def body(*refs):
        encode_kernel(*refs, count=count)

    return pl.pallas_call(
        body,
        grid=(pl.cdiv(count, BLOCK),),
        in_specs=[
            smem, smem, smem, smem, smem,
            pl.BlockSpec((BLOCK, 3, 16, 128), lambda i: (i, 0, 0, 0)),
            pl.BlockSpec((BLOCK, 16, 128), lambda i: (i, 0, 0)),
            whole, whole,
        ],
        out_specs=pl.BlockSpec((16, BLOCK, 128), lambda i: (0, i, 0)),
        out_shape=jax.ShapeDtypeStruct((16, pl.cdiv(count, BLOCK) * BLOCK, 128), BF16),
        scratch_shapes=[
            pltpu.VMEM((3, 168, 192), BF16),
            pltpu.VMEM((3, 56, 128), F32),
            pltpu.VMEM((3, 56, 128), F32),
            pltpu.VMEM((BLOCK * 16, 128), F32),
        ],
        name="encode",
    )(
        tile_idx, stencil_w.reshape(-1), depth_gain.reshape(-1), bias.reshape(-1), readout,
        snapshots, halo, classes, near_classes,
    )


def split(x):
    high = x.astype(BF16)
    return high, (x - high.astype(F32)).astype(BF16)


def lhs3(x):
    high, low = split(x)
    return jnp.concatenate([high, high, low], axis=1)


def rhs3(x):
    high, low = split(x)
    return jnp.concatenate([high, low, high], axis=1)


def dot_nt(a, b):
    return lax.dot_general(a, b, (((1,), (1,)), ((), ())), preferred_element_type=F32)


def factor_diag(block, eye):
    row8 = lax.broadcasted_iota(jnp.int32, (8, EDGE), 0)
    groups = EDGE // 8
    a = [block[8 * g : 8 * (g + 1)] for g in range(groups)]
    b = [eye[8 * g : 8 * (g + 1)] for g in range(groups)]

    def lanes(x, j):
        return jnp.broadcast_to(x[:, j : j + 1], (8, EDGE))

    def sublanes(x, i):
        return jnp.broadcast_to(x[i : i + 1, :], (8, EDGE))

    for home in range(groups):
        at = 8 * home
        cols = [lanes(a[home], at + k) for k in range(8)]
        e = [[sublanes(cols[k], i) for k in range(i + 1)] for i in range(8)]
        root = []
        mult = [[None] * 8 for _ in range(8)]
        for k in range(8):
            root.append(lax.rsqrt(e[k][k]))
            for i in range(k + 1, 8):
                mult[i][k] = e[i][k] * root[k]
            for i in range(k + 1, 8):
                for j in range(k + 1, i + 1):
                    e[i][j] = e[i][j] - mult[i][k] * mult[j][k]

        def forward(rows):
            for k in range(8):
                for m in range(k):
                    rows[k] = rows[k] - mult[k][m] * rows[m]
                rows[k] = rows[k] * root[k]
            return rows

        def pack(rows):
            out = rows[0]
            for k in range(1, 8):
                out = jnp.where(row8 == k, rows[k], out)
            return out

        u = forward([sublanes(a[home], k) for k in range(8)])
        v = forward([sublanes(b[home], k) for k in range(8)])
        a[home] = pack(u)
        b[home] = pack(v)
        for g in range(home + 1, groups):
            c = forward([lanes(a[g], at + k) for k in range(8)])
            for k in range(8):
                a[g] = a[g] - c[k] * u[k]
                b[g] = b[g] - c[k] * v[k]
    return jnp.concatenate(a, axis=0), jnp.concatenate(b, axis=0)


def pick_kernel(start_ref, enc_ref, keep_ref, near_ref, top_ref, bottom_ref):
    snaps = enc_ref.shape[1]
    pairs = start_ref.shape[1]
    snap_idx = lax.broadcasted_iota(jnp.int32, (snaps, pairs), 0)
    hit = jnp.where(snap_idx == start_ref[...], 1.0, 0.0).astype(BF16)
    panel = jnp.concatenate(
        [keep_ref[r] + near_ref[r] for r in range(keep_ref.shape[0])], axis=1
    )
    tn = (((0,), (0,)), ((), ()))
    chosen = lax.dot_general(panel, hit, tn, preferred_element_type=F32).astype(BF16)
    top_ref[...] = chosen[0:HALF]
    bottom_ref[0:HALF, :] = chosen[HALF:]
    norms = jnp.zeros(enc_ref.shape[1:], F32)
    for r in range(enc_ref.shape[0]):
        value = enc_ref[r].astype(F32)
        norms = norms + value * value
    total = jnp.zeros((enc_ref.shape[2], pairs), F32)
    for _ in range(3):
        high = norms.astype(BF16)
        total = total + lax.dot_general(high, hit, tn, preferred_element_type=F32)
        norms = norms - high.astype(F32)
    total = jnp.sum(jnp.sum(total, axis=0, keepdims=True), axis=1, keepdims=True)
    rest = jnp.broadcast_to(total, (16, pairs))
    row = lax.broadcasted_iota(jnp.int32, (16, pairs), 0)
    packed = jnp.zeros((16, pairs), BF16)
    for k in range(3):
        high = rest.astype(BF16)
        packed = jnp.where(row == k, high.astype(F32), packed.astype(F32)).astype(BF16)
        rest = rest - high.astype(F32)
    starts = start_ref[...]
    coarse = lax.shift_right_logical(starts, 2)
    for k, value in ((3, coarse), (4, starts - 4 * coarse)):
        packed = jnp.where(row == k, value.astype(F32), packed.astype(F32)).astype(BF16)
    bottom_ref[HALF:, :] = packed


def pick(starts, enc, keep, near):
    pairs = starts.shape[1]
    return pl.pallas_call(
        pick_kernel,
        out_shape=[
            jax.ShapeDtypeStruct((HALF, pairs), BF16),
            jax.ShapeDtypeStruct((HALF + 16, pairs), BF16),
        ],
        compiler_params=pltpu.CompilerParams(vmem_limit_bytes=40 * 2**20),
        name="pick_pairs",
    )(starts, enc, keep, near)


def blocks_of(flip, refs):
    top, bottom, near_top, near_bottom = refs
    mine = jnp.concatenate([top[0], bottom[0, 0:HALF, :]], axis=0)
    near = jnp.concatenate([near_top[0], near_bottom[0, 0:HALF, :]], axis=0)
    return jnp.where(flip, near, mine), jnp.where(flip, mine, near)


def gram_step(tile_ref, pieces, low_ref, power_ref):
    flip = tile_ref[0] == 1
    pairs = [blocks_of(flip, refs) for refs in pieces]
    lead = jnp.concatenate([pair[0] for pair in pairs], axis=1)
    tail = jnp.concatenate([pair[1] for pair in pairs], axis=1)
    low_ref[PANEL:, 0:PANEL] += dot_nt(tail, lead)
    for base, part in ((0, lead), (PANEL, tail)):
        low_ref[base : base + PANEL, base : base + HALF] += dot_nt(part, part[0:HALF])
        low_ref[base + HALF : base + PANEL, base + HALF : base + PANEL] += dot_nt(
            part[HALF:], part[HALF:]
        )

    @pl.when(pl.program_id(1) == 0)
    def _():
        for refs in pieces:
            for ref in (refs[1], refs[3]):
                part = ref[0, HALF:, 0:EDGE].astype(F32)
                part = part[0:1] + part[1:2] + part[2:3]
                power_ref[...] += jnp.broadcast_to(part, power_ref.shape)


def grouped(refs):
    return [refs[4 * k : 4 * (k + 1)] for k in range(len(refs) // 4)]


def gram_kernel(tile_ref, *refs):
    pieces, (low_ref, power_ref) = refs[:-2], refs[-2:]

    @pl.when(at_step(0, 0))
    def _():
        low_ref[...] = jnp.zeros(low_ref.shape, F32)
        power_ref[...] = jnp.zeros(power_ref.shape, F32)

    gram_step(tile_ref, grouped(pieces), low_ref, power_ref)


def factor_kernel(tile_ref, sums_ref, energy_ref, *refs, pairs_total, obs):
    pieces, (low_ref, inv_ref, out_ref, shift_ref) = refs[:-4], refs[-4:]

    @pl.when(at_step(0, 0))
    def _():
        low_ref[...] = sums_ref[...]
        shift_ref[...] = energy_ref[...]

    gram_step(tile_ref, grouped(pieces), low_ref, shift_ref)

    @pl.when(at_step(pl.num_programs(0) - 1, SPLIT - 1))
    def _():
        shift = 0.5 * (shift_ref[...] / pairs_total) / float(obs)
        out_ref[0, 0] = shift[0, 0]
        factor(low_ref, inv_ref, shift, 1.0 / pairs_total)


def factor(low_ref, inv_ref, shift, scale):
    width = low_ref.shape[0]
    row = lax.broadcasted_iota(jnp.int32, (EDGE, EDGE), 0)
    col = lax.broadcasted_iota(jnp.int32, (EDGE, EDGE), 1)
    eye = jnp.where(row == col, 1.0, 0.0)
    blocks = width // EDGE
    shift_wide = jnp.concatenate([shift] * (EDGE // 8), axis=0)

    for i in range(blocks):
        rows = pl.ds(EDGE * i, EDGE)
        low_ref[rows, :] = low_ref[rows, :] * scale
        low_ref[rows, EDGE * i : EDGE * (i + 1)] += jnp.where(row == col, shift_wide, 0.0)
        if EDGE * (i + 1) < width:
            low_ref[rows, EDGE * (i + 1) :] = jnp.zeros((EDGE, width - EDGE * (i + 1)), F32)

    def update(k):
        here = EDGE * k
        rest = EDGE * (k + 1)
        below = dot_nt(lhs3(low_ref[rest:, here:rest]), rhs3(inv_ref[here:rest, :]))
        low_ref[rest:, here:rest] = below
        left = lhs3(below)
        right = rhs3(below)
        start = rest
        while start < width:
            stop = start + (2 * EDGE if (width - start) % (2 * EDGE) == 0 else EDGE)
            low_ref[start:, start:stop] -= dot_nt(
                left[start - rest :], right[start - rest : stop - rest]
            )
            start = stop

    def step(k, carry):
        at = pl.ds(pl.multiple_of(k * EDGE, EDGE), EDGE)
        upper, inverse = factor_diag(low_ref[at, at], eye)
        low_ref[at, at] = jnp.where(col >= row, upper, 0.0).T
        inv_ref[at, :] = inverse
        for static in range(blocks - 1):
            @pl.when(k == static)
            def _():
                update(static)
        return carry

    lax.fori_loop(0, blocks, step, 0)
    for i in range(blocks - 1):
        low_ref[EDGE * i : EDGE * (i + 1), EDGE * (i + 1) : EDGE * (i + 2)] = jnp.zeros((EDGE, EDGE), F32)


SPLIT = 1


def whole(shape):
    return pl.BlockSpec(shape, lambda i, j: (0,) * len(shape))


def piece_specs(pieces):
    return [
        pl.BlockSpec((1, piece.shape[1], piece.shape[2] // SPLIT), lambda i, j: (i, 0, j))
        for piece in pieces
    ]


def at_step(i, j):
    return (pl.program_id(0) == i) & (pl.program_id(1) == j)


SUMS = jax.ShapeDtypeStruct((2 * PANEL, 2 * PANEL), F32)
POWER = jax.ShapeDtypeStruct((8, EDGE), F32)
LIMIT = pltpu.CompilerParams(vmem_limit_bytes=56 * 2**20)


def gram_part(tile_idx, pieces):
    return pl.pallas_call(
        gram_kernel,
        grid=(pieces[0].shape[0], SPLIT),
        in_specs=[pl.BlockSpec(memory_space=pltpu.SMEM)] + piece_specs(pieces),
        out_specs=[whole(SUMS.shape), whole(POWER.shape)],
        out_shape=[SUMS, POWER],
        compiler_params=LIMIT,
        cost_estimate=pl.CostEstimate(
            flops=6 * PANEL**2 * 4 * pieces[0].shape[0] * PANEL,
            transcendentals=0,
            bytes_accessed=sum(2 * x.size for x in pieces) + 4 * SUMS.size,
        ),
        name="gram_part",
    )(tile_idx, *pieces)


def gram_factor(tile_idx, sums, energy, pieces, pairs_total, obs):
    def body(*refs):
        factor_kernel(*refs, pairs_total=pairs_total, obs=obs)

    return pl.pallas_call(
        body,
        grid=(pieces[0].shape[0], SPLIT),
        in_specs=[pl.BlockSpec(memory_space=pltpu.SMEM), whole(SUMS.shape), whole(POWER.shape)]
        + piece_specs(pieces),
        out_specs=[
            whole(SUMS.shape),
            whole((2 * PANEL, EDGE)),
            pl.BlockSpec(memory_space=pltpu.SMEM),
        ],
        out_shape=[
            SUMS,
            jax.ShapeDtypeStruct((2 * PANEL, EDGE), F32),
            jax.ShapeDtypeStruct((1, 1), F32),
        ],
        scratch_shapes=[pltpu.VMEM(POWER.shape, F32)],
        compiler_params=LIMIT,
        name="gram_factor",
    )(tile_idx, sums, energy, *pieces)


def rows_kernel(info_ref, enc_ref, low_ref, inv_ref, *refs, pairs_total):
    pieces, (chol_ref, white_ref, sums_ref) = refs[:-3], refs[-3:]
    step = pl.program_id(0)
    own = chol_ref.shape[0]
    width = 2 * PANEL

    @pl.when(at_step(0, 0))
    def _():
        sums_ref[...] = jnp.zeros(sums_ref.shape, F32)

    snaps = enc_ref.shape[1]
    pairs = pieces[0].shape[2]
    snap_idx = lax.broadcasted_iota(jnp.int32, (snaps, pairs), 0)
    tn = (((0,), (0,)), ((), ()))
    flip = info_ref[0] == 1
    top_bit = enc_ref.shape[0] // 2
    parts = grouped(pieces)
    picked = []
    for k in range(len(parts)):
        source = jnp.bitwise_xor(info_ref[4], (k // 4) * top_bit + step * 4 + k % 4)
        values = enc_ref[source]
        packed = parts[k][1][0, HALF:, :].astype(F32)
        starts = (4.0 * packed[3:4] + packed[4:5]).astype(jnp.int32)
        hit = jnp.where(snap_idx == starts, 1.0, 0.0).astype(BF16)
        following = pltpu.roll(values.astype(F32), snaps - 1, 0).astype(BF16)
        if own % EDGE == 0:
            wide = jnp.concatenate([values, following], axis=1)
            rows = lax.dot_general(wide, hit, tn, preferred_element_type=F32)
        else:
            rows = jnp.concatenate(
                [
                    lax.dot_general(values, hit, tn, preferred_element_type=F32),
                    lax.dot_general(following, hit, tn, preferred_element_type=F32),
                ],
                axis=0,
            )
        picked.append(rows.astype(BF16))
    both = [blocks_of(flip, part) for part in parts]
    picked = jnp.concatenate(picked, axis=1)
    sums_ref[:, 0:PANEL] += dot_nt(picked, jnp.concatenate([b[0] for b in both], axis=1))
    sums_ref[:, PANEL:] += dot_nt(picked, jnp.concatenate([b[1] for b in both], axis=1))

    @pl.when(at_step(pl.num_programs(0) - 1, SPLIT - 1))
    def _():
        sums_ref[...] = sums_ref[...] * (1.0 / pairs_total)
        for k in range(width // EDGE):
            here = EDGE * k
            rest = EDGE * (k + 1)
            solved = dot_nt(lhs3(sums_ref[:, here:rest]), rhs3(inv_ref[here:rest, :]))
            sums_ref[:, here:rest] = solved
            if rest < width:
                sums_ref[:, rest:] -= dot_nt(lhs3(solved), rhs3(low_ref[rest:, here:rest]))
        offset = info_ref[3]
        first_rows = low_ref[pl.ds(pl.multiple_of(offset, 8), own), :]
        second_rows = low_ref[pl.ds(pl.multiple_of(PANEL + offset, 8), own), :]
        chol_ref[...] = jnp.where(
            info_ref[1] == 1,
            first_rows,
            jnp.where(info_ref[2] == 1, second_rows, sums_ref[0:own, :]),
        )
        white_ref[...] = sums_ref[own:, :]


def whiten_rows(info, enc, low, inv, pieces, pairs_total):
    own = enc.shape[2]
    width = 2 * PANEL

    def body(*refs):
        rows_kernel(*refs, pairs_total=pairs_total)

    return pl.pallas_call(
        body,
        grid=(pieces[0].shape[0], SPLIT),
        in_specs=[pl.BlockSpec(memory_space=pltpu.SMEM)]
        + [whole(x.shape) for x in (enc, low, inv)]
        + piece_specs(pieces),
        out_specs=[whole((own, width))] * 2,
        out_shape=[jax.ShapeDtypeStruct((own, width), F32)] * 2,
        scratch_shapes=[pltpu.VMEM((2 * own, width), F32)],
        compiler_params=LIMIT,
        name="whiten_rows",
    )(info, enc, low, inv, *pieces)


def after_kernel(value_ref, *refs):
    del value_ref, refs


def after(value, *earlier):
    hbm = pl.BlockSpec(memory_space=pl.ANY)
    return pl.pallas_call(
        after_kernel,
        in_specs=[hbm] * (1 + len(earlier)),
        out_specs=hbm,
        out_shape=jax.ShapeDtypeStruct(value.shape, value.dtype),
        input_output_aliases={0: 0},
        name="after",
    )(value, *earlier)


def gather_pieces(parts, dp_count, swap, tile_idx):
    def across(arrays, bit):
        pairs = [(i, i ^ bit) for i in range(dp_count)]
        return [lax.ppermute(x, "dp", pairs) for x in arrays]

    top_bit = dp_count // 2
    chunks = []
    sums = None
    for start in (parts, across(parts, top_bit)):
        bit = 4
        while bit < top_bit:
            far = across(start, bit)
            start = [jnp.concatenate(pair, axis=0) for pair in zip(start, far)]
            bit *= 2
        top, bottom = start
        (top_x,) = across([top], 1)
        (bottom_y,) = across([bottom], 2)
        (top_y,) = across([top], 2)
        (bottom_x,) = across([bottom], 1)
        (top_xy,) = across([top_x], 2)
        (bottom_xy,) = across([bottom_y], 1)
        if sums is not None:
            top_xy = after(top_xy, *sums)
        pieces = []
        for pair in ((top, bottom), (top_x, bottom_x), (top_y, bottom_y), (top_xy, bottom_xy)):
            pieces.extend(pair)
            pieces.extend(lax.ppermute(x, "tile", swap) for x in pair)
        chunks.append(pieces)
        if sums is None:
            sums = gram_part(tile_idx, pieces)
    return chunks, sums


def on_device(
    snapshots, pair_start, bath_class, stencil_w, depth_gain, stencil_bias, readout, panel_order
):
    tile_pos = lax.axis_index("tile")
    dp_pos = lax.axis_index("dp")
    tile_count = lax.axis_size("tile")
    dp_count = lax.axis_size("dp")
    grid_rows, grid_cols = bath_class.shape
    tile_obs = grid_rows * grid_cols
    own_rows = tile_obs // dp_count
    swap = [(0, 1), (1, 0)]
    tile_idx = tile_pos[None].astype(jnp.int32)

    near_class = lax.ppermute(bath_class, "tile", swap)
    halo = lax.ppermute(halo_rows(tile_idx, snapshots), "tile", swap)
    encoded = encode(
        tile_idx, snapshots, halo, bath_class, near_class,
        stencil_w, depth_gain, stencil_bias, readout,
    )
    snaps = encoded.shape[1]

    block_rows = PANEL // grid_cols
    tile_blocks = tile_obs // PANEL

    def block_part(block):
        at = (block % tile_blocks) * block_rows
        part = lax.dynamic_slice_in_dim(encoded, at, block_rows, 0)
        return jnp.where(block // tile_blocks == tile_pos, part, jnp.zeros((), BF16))

    keep = block_part(jnp.where(tile_pos == 0, panel_order[0], panel_order[1]))
    send = block_part(jnp.where(tile_pos == 0, panel_order[1], panel_order[0]))
    own_parts = pick(pair_start[None, :], encoded, keep, lax.ppermute(send, "tile", swap))
    chunks, sums = gather_pieces([part[None] for part in own_parts], dp_count, swap, tile_idx)

    by_owner = encoded
    if own_rows != grid_cols:
        by_owner = encoded.reshape(grid_rows, snaps, grid_cols // own_rows, own_rows)
        by_owner = by_owner.transpose(0, 2, 1, 3).reshape(dp_count, snaps, own_rows)
    by_owner = after(by_owner, *chunks[0], *chunks[1])
    own_enc = lax.all_to_all(by_owner, "dp", 0, 0, tiled=False)

    pairs_total = float(pair_start.shape[0] * dp_count)
    low, inv, shift = gram_factor(
        tile_idx, *sums, chunks[1], pairs_total, tile_obs * tile_count
    )
    grow_start = tile_pos * tile_obs + dp_pos * own_rows
    own_block = grow_start // PANEL
    info = jnp.stack(
        [
            tile_pos,
            (own_block == panel_order[0]).astype(jnp.int32),
            (own_block == panel_order[1]).astype(jnp.int32),
            grow_start - own_block * PANEL,
            dp_pos,
        ]
    ).astype(jnp.int32)
    factor_rows, whitened = whiten_rows(
        info, own_enc, low, inv, chunks[0] + chunks[1], pairs_total
    )
    return (factor_rows[None], whitened[None], shift.reshape(()))


def solution(mesh):
    placed = (P("dp", None, "tile", None), P("dp"), P("tile", None), P(), P(), P(), P(), P())
    return jax.shard_map(
        on_device,
        mesh=mesh,
        in_specs=placed,
        out_specs=(P("tile", "dp", None), P("tile", "dp", None), P()),
        check_vma=False,
    )
```
